512 devices in a mesh: row: 16 (over z_hi, x), col: 32 (over y, z_lo, core).
Axes of the slice: x: 4, y: 4, z: 16 (z_hi: 4, z_lo: 4; z = z_hi * 4 + z_lo), core: 2. Of those that a mesh axis runs over, the one named last changes fastest.
Arguments:
- features: bfloat16 [64, 2048, 2048], P(None, 'col', 'row'), may hold values from -6 to 6
- conv_weight: bfloat16 [3, 3, 64, 64], replicated, may hold values from -0.25 to 0.25
- conv_bias: float32 [64], replicated, may hold values from -3 to 3
- head_weight: bfloat16 [62, 64], replicated, may hold values from -40 to 40
- head_bias: float32 [62], replicated, may hold values from -4 to 4
- dist_label: int32 [2048, 2048], P('col', 'row'), may hold values from 0 to 36, as said below
- omega_label: int32 [2048, 2048], P('col', 'row'), may hold values from 0 to 24, as said below
- residue_mask: int32 [2048], replicated, may hold values from 0 to 1, as said below
Outputs:
- grad_input: bfloat16 [64, 2048, 2048], P(None, 'col', 'row')
- grad_conv_weight: float32 [3, 3, 64, 64], replicated
- grad_conv_bias: float32 [64], replicated
- grad_head_weight: float32 [62, 64], replicated
- grad_head_bias: float32 [62], replicated
The draws below stay inside these ranges and needn't reach their ends.
Inputs may be any that keep to these rules, and one draw needn't show every extreme that they name: dist_label[i, j] = dist_label[j, i]. omega_label[i, j] = omega_label[j, i]. `residue_mask`: at least one residue has coordinates.
All inputs are finite; a program needn't handle non-finite values.
Results may differ from the reference program's by a relative error of at most 0.0025.
The reference program's roundings to bfloat16 on the way (of `act`, `mixed`, `logits`, `grad_logit` and `grad_pre`) count: a program that leaves them out, or rounds other values in their place, can miss the bound.
Values may be sent and summed in bfloat16 or wider, within the bound.
A program may use at most 64 MiB of HBM per device.

```python
import math
import jax
import jax.numpy as jnp
from jax import lax

C = 64
DILATION_STEP = 16
DB = 37
OB = 25
L = 2048
NB = 62


def symmetric_labels(key, bins):
    upper = jax.random.randint(key, (L, L), 0, bins, dtype=jnp.int32)
    index_position = jnp.arange(L, dtype=jnp.int32)
    return jnp.where(index_position[:, None] <= index_position[None, :], upper, upper.T)


def draw_dist_label(key, part):
    return symmetric_labels(jax.random.fold_in(key, 11), DB)


def draw_omega_label(key, part):
    return symmetric_labels(jax.random.fold_in(key, 23), OB)


def draw_residue_mask(key, part):
    first_member, second_member = jax.random.split(jax.random.fold_in(key, 53))
    levels = jax.random.randint(first_member, (L,), 0, 10, dtype=jnp.int32)
    chosen = jax.random.randint(second_member, (), 0, L, dtype=jnp.int32)
    index_position = jnp.arange(L, dtype=jnp.int32)
    present = jnp.where(levels < 9, 1, 0).astype(jnp.int32)
    return jnp.where(index_position == chosen, 1, present).astype(jnp.int32)


def draw_head_weight(key, part):
    first_member = jax.random.fold_in(jax.random.fold_in(key, 37), 0)
    base = jnp.clip(jax.random.normal(first_member, (NB, C), jnp.float32), -6.0, 6.0)
    base = base / math.sqrt(C)
    return base.astype(jnp.bfloat16)


def block_scale(stream_key, shape, pieces, smallest, largest):
    def one(axis_at, shards_of):
        steps = jax.random.uniform(jax.random.fold_in(jax.random.fold_in(stream_key, 6), axis_at), (shards_of,), jnp.float32, smallest / len(pieces), largest / len(pieces))
        return jnp.repeat(jnp.exp(steps), shape[axis_at] // shards_of).reshape((-1,) + (1,) * (len(shape) - axis_at - 1))

    factor_of = one(*pieces[0])
    for cut in pieces[1:]:
        factor_of = factor_of * one(*cut)
    return factor_of


def gaussian(own_key, dims, deviation, reach, shards=(), kind=jnp.bfloat16):
    entries = deviation * jax.random.normal(own_key, dims, jnp.float32)
    if shards:
        entries = entries * block_scale(own_key, dims, shards, -0.22, 0.18)
    return jnp.clip(entries, -reach, reach).astype(kind)


def setup_inputs(seed: int = 0) -> dict:
    arg_keys = jax.random.split(jax.random.key(seed), 9)
    return {
        "features": gaussian(arg_keys[0], (C, L, L), 1.0, 6.0, ((1, 32), (2, 16))),
        "conv_weight": gaussian(arg_keys[1], (3, 3, C, C), (9 * C) ** -0.5, 0.25),
        "conv_bias": gaussian(arg_keys[2], (C,), 0.5, 3.0, (), jnp.float32),
        "head_weight": draw_head_weight(jax.random.fold_in(arg_keys[8], 71), 0),
        "head_bias": gaussian(arg_keys[4], (NB,), 1.0, 4.0, (), jnp.float32),
        "dist_label": draw_dist_label(jax.random.fold_in(arg_keys[8], 71), 0),
        "omega_label": draw_omega_label(jax.random.fold_in(arg_keys[8], 71), 0),
        "residue_mask": draw_residue_mask(jax.random.fold_in(arg_keys[8], 71), 0),
    }


def dilated(padded_input, weight):
    block_size = padded_input.shape[1] - 2 * DILATION_STEP
    block_tile = math.gcd(block_size, 256)
    count = block_size // block_tile
    w32 = weight.astype(jnp.float32)

    def one(index_position):
        row_band = lax.dynamic_slice_in_dim(padded_input, index_position * block_tile, block_tile + 2 * DILATION_STEP, 1).astype(jnp.float32)
        total = jnp.zeros((weight.shape[2], block_tile, block_size), jnp.float32)
        for first_member in range(3):
            for second_member in range(3):
                part = row_band[:, first_member * DILATION_STEP:first_member * DILATION_STEP + block_tile, second_member * DILATION_STEP:second_member * DILATION_STEP + block_size]
                total = total + jnp.einsum('oc,cxy->oxy', w32[first_member, second_member], part)
        return total
    out = lax.map(one, jnp.arange(count, dtype=jnp.int32))
    return jnp.transpose(out, (1, 0, 2, 3)).reshape(weight.shape[2], block_size, block_size)

def weight_terms(grad_pre, padded_input):
    block_size = grad_pre.shape[1]
    block_tile = math.gcd(block_size, 256)
    count = block_size // block_tile

    def one(index_position):
        row_band = lax.dynamic_slice_in_dim(padded_input, index_position * block_tile, block_tile + 2 * DILATION_STEP, 1).astype(jnp.float32)
        block = lax.dynamic_slice_in_dim(grad_pre, index_position * block_tile, block_tile, 1).astype(jnp.float32)
        rows_out = []
        for first_member in range(3):
            cols_out = []
            for second_member in range(3):
                part = row_band[:, first_member * DILATION_STEP:first_member * DILATION_STEP + block_tile, second_member * DILATION_STEP:second_member * DILATION_STEP + block_size]
                cols_out.append(jnp.einsum('oxy,cxy->oc', block, part))
            rows_out.append(jnp.stack(cols_out, 0))
        return jnp.stack(rows_out, 0)
    return lax.optimization_barrier(jnp.sum(lax.map(one, jnp.arange(count, dtype=jnp.int32)), axis=0))

def group_grad(scores, labels):
    prob = jax.nn.softmax(scores, axis=0)
    onehot = (jnp.arange(scores.shape[0], dtype=jnp.int32)[:, None, None] == labels[None]).astype(jnp.float32)
    return prob - onehot

def reference(features, conv_weight, conv_bias, head_weight, head_bias, dist_label, omega_label, residue_mask):
    padding_widths = ((0, 0), (DILATION_STEP, DILATION_STEP), (DILATION_STEP, DILATION_STEP))
    x32 = features.astype(jnp.float32)
    act = jax.nn.elu(x32).astype(jnp.bfloat16)
    act_pad = jnp.pad(act, padding_widths)
    pre = dilated(act_pad, conv_weight) + conv_bias[:, None, None]
    mixed = (x32 + pre).astype(jnp.bfloat16)
    head32 = head_weight.astype(jnp.float32)
    mixed32 = mixed.astype(jnp.float32)
    logits = (jnp.einsum('nc,cxy->nxy', head32, mixed32) + head_bias[:, None, None]).astype(jnp.bfloat16)
    logit32 = logits.astype(jnp.float32)
    sym = 0.5 * (logit32 + jnp.transpose(logit32, (0, 2, 1)))
    mask = residue_mask.astype(jnp.float32)
    pair = mask[:, None] * mask[None, :]
    count = jnp.sum(mask)
    grad_sym = jnp.concatenate([group_grad(sym[:DB], dist_label), group_grad(sym[DB:], omega_label)], axis=0) * pair[None]
    grad_logit = (0.5 * (grad_sym + jnp.transpose(grad_sym, (0, 2, 1)))).astype(jnp.bfloat16)
    grad_logit32 = grad_logit.astype(jnp.float32)
    grad_mixed = jnp.einsum('nc,nxy->cxy', head32, grad_logit32)
    grad_head_weight = jnp.einsum('nxy,cxy->nc', grad_logit32, mixed32) / count
    grad_head_bias = lax.optimization_barrier(jnp.sum(grad_sym, axis=(1, 2))) / count
    grad_pre = grad_mixed.astype(jnp.bfloat16)
    flipped = jnp.transpose(conv_weight[::-1, ::-1], (0, 1, 3, 2))
    grad_act = dilated(jnp.pad(grad_pre, padding_widths), flipped)
    grad_conv_weight = weight_terms(grad_pre, act_pad) / count
    grad_conv_bias = lax.optimization_barrier(jnp.sum(grad_mixed, axis=(1, 2))) / count
    slope = jnp.where(x32 > 0.0, jnp.float32(1.0), jnp.exp(jnp.minimum(x32, 0.0)))
    grad_input = (grad_mixed + slope * grad_act).astype(jnp.bfloat16)
    return (grad_input, grad_conv_weight, grad_conv_bias, grad_head_weight, grad_head_bias)
```

```python
import jax
import jax.numpy as jnp
from jax import lax
from jax.experimental import pallas as pl
from jax.experimental.pallas import tpu as pltpu
from jax.sharding import PartitionSpec as P

DILATION_STEP = 16
DB = 37

MESH = pl.DeviceIdType.MESH


def place():
    row = lax.axis_index("row")
    col = lax.axis_index("col")
    x = lax.rem(row, 4)
    zh = row // 4
    core = lax.rem(col, 2)
    q = col // 2
    y = q // 4
    zl = lax.rem(q, 4)
    return x, y, 4 * zh + zl, core


def device(x, y, z, core):
    return ((z // 4) * 4 + x, (y * 4 + lax.rem(z, 4)) * 2 + core)


def mirror_kernel(src, dst, tmp, send_a, recv_a, send_b, recv_b):
    x, y, z, core = place()
    me_k = 4 * y + x
    a_target = lambda k: (lax.rem(k, 4), k // 4, z, core)
    a_source = lambda s: (lax.rem(s, 4), s // 4, z, core)
    a_slot = me_k
    b_target = lambda s, h: (lax.rem(z, 4), z // 4, s, h)
    b_source = lambda k, c: (lax.rem(k, 4), k // 4, me_k, c)
    rot = me_k

    def is_me(t):
        return (t[0] == x) & (t[1] == y) & (t[2] == z) & (t[3] == core)

    barrier = pltpu.get_barrier_semaphore()

    def greet(t):
        @pl.when(jnp.logical_not(is_me(t)))
        def _():
            pl.semaphore_signal(barrier, inc=1, device_id=device(*t), device_id_type=MESH)

    def greet_all(s, carry):
        greet(a_source(s))
        greet(b_source(s, 0))
        greet(b_source(s, 1))
        return carry

    lax.fori_loop(0, 16, greet_all, 0)

    pl.semaphore_wait(barrier, jnp.where(me_k == z, 46, 47))

    def phase_a(t, carry):
        k = lax.rem(me_k + t, 16)
        to = a_target(k)
        for h in range(2):
            @pl.when(is_me(to))
            def _():
                pltpu.make_async_copy(src.at[h, k], tmp.at[a_slot, h], recv_a.at[a_slot, h]).start()

            @pl.when(jnp.logical_not(is_me(to)))
            def _():
                pltpu.make_async_remote_copy(
                    src_ref=src.at[h, k], dst_ref=tmp.at[a_slot, h], send_sem=send_a.at[k, h],
                    recv_sem=recv_a.at[a_slot, h], device_id=device(*to), device_id_type=MESH).start()
        return carry

    lax.fori_loop(0, 16, phase_a, 0)

    def phase_b(t, carry):
        s = lax.rem(rot + t, 16)
        for h in range(2):
            pltpu.make_async_copy(src.at[h, 0], tmp.at[s, h], recv_a.at[s, h]).wait()
            to = b_target(s, h)
            @pl.when(is_me(to))
            def _():
                pltpu.make_async_copy(tmp.at[s, h], dst.at[core, me_k], recv_b.at[core, me_k]).start()

            @pl.when(jnp.logical_not(is_me(to)))
            def _():
                pltpu.make_async_remote_copy(
                    src_ref=tmp.at[s, h], dst_ref=dst.at[core, me_k], send_sem=send_b.at[s, h],
                    recv_sem=recv_b.at[core, me_k], device_id=device(*to), device_id_type=MESH).start()
        return carry

    lax.fori_loop(0, 16, phase_b, 0)

    def finish(k, carry):
        for c in range(2):
            pltpu.make_async_copy(tmp.at[0, 0], dst.at[c, k], recv_b.at[c, k]).wait()
        for h in range(2):
            @pl.when(jnp.logical_not(is_me(a_target(k))))
            def _():
                pltpu.make_async_copy(src.at[h, k], tmp.at[0, h], send_a.at[k, h]).wait()

            @pl.when(jnp.logical_not(is_me(b_target(k, h))))
            def _():
                pltpu.make_async_copy(tmp.at[k, h], dst.at[0, 0], send_b.at[k, h]).wait()
        return carry

    lax.fori_loop(0, 16, finish, 0)


def exchange(packed):
    piece = packed.shape[2:]
    return pl.pallas_call(
        mirror_kernel,
        out_shape=jax.ShapeDtypeStruct(packed.shape, packed.dtype),
        in_specs=[pl.BlockSpec(memory_space=pltpu.VMEM)],
        out_specs=pl.BlockSpec(memory_space=pltpu.VMEM),
        scratch_shapes=[
            pltpu.VMEM((16, 2) + piece, packed.dtype),
            pltpu.SemaphoreType.DMA((16, 2)),
            pltpu.SemaphoreType.DMA((16, 2)),
            pltpu.SemaphoreType.DMA((16, 2)),
            pltpu.SemaphoreType.DMA((2, 16)),
        ],
        compiler_params=pltpu.CompilerParams(collective_id=1, has_side_effects=True),
        name="mirror",
    )(packed)


def total_kernel(src, dst, parts, mine, ring, send_1, recv_1, send_2, recv_2, send_3, recv_3):
    x, y, z, core = place()
    me_s = (4 * y + x) * 2 + core

    def plane(s):
        return (lax.rem(s // 2, 4), s // 8, z, lax.rem(s, 2))

    barrier = pltpu.get_barrier_semaphore()

    def greet_plane(t, carry):
        s = lax.rem(me_s + t, 32)
        pl.semaphore_signal(barrier, inc=1, device_id=device(*plane(s)), device_id_type=MESH)
        return carry

    def greet_ring(t, carry):
        pl.semaphore_signal(
            barrier, inc=1, device_id=device(x, y, lax.rem(z + t, 16), core), device_id_type=MESH)
        return carry

    lax.fori_loop(1, 32, greet_plane, 0)
    lax.fori_loop(1, 16, greet_ring, 0)
    pl.semaphore_wait(barrier, 46)

    def send_parts(t, carry):
        s = lax.rem(me_s + t, 32)
        pltpu.make_async_remote_copy(
            src_ref=src.at[s], dst_ref=parts.at[me_s], send_sem=send_1.at[s],
            recv_sem=recv_1.at[me_s], device_id=device(*plane(s)), device_id_type=MESH).start()
        return carry

    lax.fori_loop(1, 32, send_parts, 0)

    def wait_parts(t, carry):
        s = lax.rem(me_s + t, 32)
        pltpu.make_async_copy(src.at[0], parts.at[s], recv_1.at[s]).wait()
        return carry

    parts[me_s] = src[me_s]
    lax.fori_loop(1, 32, wait_parts, 0)
    mine[...] = jnp.sum(parts[...], axis=0)
    ring[z] = mine[...]

    def send_ring(t, carry):
        o = lax.rem(z + t, 16)
        pltpu.make_async_remote_copy(
            src_ref=mine, dst_ref=ring.at[z], send_sem=send_2.at[o],
            recv_sem=recv_2.at[z], device_id=device(x, y, o, core), device_id_type=MESH).start()
        return carry

    lax.fori_loop(1, 16, send_ring, 0)

    def wait_ring(t, carry):
        o = lax.rem(z + t, 16)
        pltpu.make_async_copy(mine, ring.at[o], recv_2.at[o]).wait()
        pltpu.make_async_copy(mine, ring.at[o], send_2.at[o]).wait()
        return carry

    lax.fori_loop(1, 16, wait_ring, 0)
    mine[...] = jnp.sum(ring[...], axis=0)
    dst[me_s] = mine[...]

    def send_all(t, carry):
        s = lax.rem(me_s + t, 32)
        pltpu.make_async_remote_copy(
            src_ref=mine, dst_ref=dst.at[me_s], send_sem=send_3.at[s],
            recv_sem=recv_3.at[me_s], device_id=device(*plane(s)), device_id_type=MESH).start()
        return carry

    lax.fori_loop(1, 32, send_all, 0)

    def finish(t, carry):
        s = lax.rem(me_s + t, 32)
        pltpu.make_async_copy(mine, dst.at[s], recv_3.at[s]).wait()
        pltpu.make_async_copy(mine, dst.at[s], send_3.at[s]).wait()
        pltpu.make_async_copy(mine, dst.at[s], send_1.at[s]).wait()
        return carry

    lax.fori_loop(1, 32, finish, 0)


def total(values):
    return pl.pallas_call(
        total_kernel,
        out_shape=jax.ShapeDtypeStruct(values.shape, values.dtype),
        in_specs=[pl.BlockSpec(memory_space=pltpu.VMEM)],
        out_specs=pl.BlockSpec(memory_space=pltpu.VMEM),
        scratch_shapes=[
            pltpu.VMEM(values.shape, values.dtype),
            pltpu.VMEM(values.shape[1:], values.dtype),
            pltpu.VMEM((16,) + values.shape[1:], values.dtype),
            pltpu.SemaphoreType.DMA((32,)),
            pltpu.SemaphoreType.DMA((32,)),
            pltpu.SemaphoreType.DMA((16,)),
            pltpu.SemaphoreType.DMA((16,)),
            pltpu.SemaphoreType.DMA((32,)),
            pltpu.SemaphoreType.DMA((32,)),
        ],
        compiler_params=pltpu.CompilerParams(collective_id=2, has_side_effects=True),
        name="total",
    )(values)


def with_halo(cells, sides, width):
    for axis, dim in sides:
        count = lax.axis_size(axis)
        ends = count - 1
        head = lax.slice_in_dim(cells, 0, width, axis=dim)
        tail = lax.slice_in_dim(cells, cells.shape[dim] - width, cells.shape[dim], axis=dim)
        cells = jnp.concatenate(
            [
                lax.ppermute(tail, axis, [(i, (i + 1) % count) for i in range(ends)]),
                cells,
                lax.ppermute(head, axis, [((i + 1) % count, i) for i in range(ends)]),
            ],
            axis=dim,
        )
    return cells


def extend(receptive_field, which):
    if which == "act":
        return with_halo(receptive_field, (("col", 1), ("row", 2)), DILATION_STEP)
    return with_halo(receptive_field, (("col", 1), ("row", 2)), DILATION_STEP)


def tap_stack(extended_input, first_member, row_span, column_span):
    start = first_member * DILATION_STEP
    band = extended_input[:, start : start + row_span, :]
    pieces = [
        band[:, :, second_member * DILATION_STEP : second_member * DILATION_STEP + column_span]
        for second_member in range(3)
    ]
    return jnp.concatenate(pieces, axis=0)


def tap_matrix(weight, first_member):
    channels_out = weight.shape[2]
    channels_in = weight.shape[3]
    return jnp.transpose(weight[first_member], (1, 0, 2)).reshape(channels_out, 3 * channels_in)


def dilated(extended_input, weight, row_span, column_span):
    total = None
    for first_member in range(3):
        stacked = tap_stack(extended_input, first_member, row_span, column_span)
        term = jnp.einsum(
            "ok,kxy->oxy",
            tap_matrix(weight, first_member),
            stacked,
            preferred_element_type=jnp.float32,
        )
        total = term if total is None else total + term
    return total


def mirror(logits):
    bins, row_span, column_span = logits.shape
    padded = jnp.pad(logits, ((0, 64 - bins), (0, 0), (0, 0)))
    packed = jnp.transpose(padded.reshape(2, 32, row_span, 2, 64), (3, 1, 2, 0, 4))
    placed = exchange(packed.reshape(2, 16, 2, row_span, 128)).reshape(2, 32, row_span, 2, 64)
    return jnp.transpose(placed, (3, 1, 4, 0, 2)).reshape(64, row_span, column_span)[:bins]


def group_grad(scores, labels):
    prob = jax.nn.softmax(scores, axis=0)
    onehot = (jnp.arange(scores.shape[0], dtype=jnp.int32)[:, None, None] == labels[None]).astype(
        jnp.float32
    )
    return prob - onehot


def per_device(
    features, conv_weight, conv_bias, head_weight, head_bias, dist_label, omega_label, residue_mask
):
    channels, row_span, column_span = features.shape
    x32 = features.astype(jnp.float32)
    act = jax.nn.elu(x32).astype(jnp.bfloat16)
    activation_extended = extend(act, "act")
    pre = (
        dilated(activation_extended, conv_weight, row_span, column_span) + conv_bias[:, None, None]
    )
    mixed = (x32 + pre).astype(jnp.bfloat16)
    logits = (
        jnp.einsum("nc,cxy->nxy", head_weight, mixed, preferred_element_type=jnp.float32)
        + head_bias[:, None, None]
    ).astype(jnp.bfloat16)
    mirrored = mirror(logits)
    sym = 0.5 * (logits.astype(jnp.float32) + mirrored.astype(jnp.float32))
    mask = residue_mask.astype(jnp.float32)
    mask_first = lax.dynamic_slice_in_dim(mask, lax.axis_index("col") * row_span, row_span)
    mask_second = lax.dynamic_slice_in_dim(mask, lax.axis_index("row") * column_span, column_span)
    pair = mask_first[:, None] * mask_second[None, :]
    count = jnp.sum(mask)
    grad_sym = (
        jnp.concatenate(
            [group_grad(sym[:DB], dist_label), group_grad(sym[DB:], omega_label)], axis=0
        )
        * pair[None]
    )
    grad_logit = grad_sym.astype(jnp.bfloat16)
    grad_mixed = jnp.einsum(
        "nc,nxy->cxy", head_weight, grad_logit, preferred_element_type=jnp.float32
    )
    head_w_term = jnp.einsum("nxy,cxy->nc", grad_logit, mixed, preferred_element_type=jnp.float32)
    head_b_term = jnp.sum(grad_sym, axis=(1, 2))
    grad_pre = grad_mixed.astype(jnp.bfloat16)
    grad_wide = extend(grad_pre, "grad")
    flipped = jnp.transpose(conv_weight[::-1, ::-1], (0, 1, 3, 2))
    grad_act = dilated(grad_wide, flipped, row_span, column_span)
    tap_rows = []
    for first_member in range(3):
        stacked = tap_stack(activation_extended, first_member, row_span, column_span)
        flat = jnp.einsum("oxy,kxy->ok", grad_pre, stacked, preferred_element_type=jnp.float32)
        tap_rows.append(jnp.transpose(flat.reshape(channels, 3, channels), (1, 0, 2)))
    conv_w_term = jnp.stack(tap_rows, 0)
    conv_b_term = jnp.sum(grad_mixed, axis=(1, 2))
    flat = jnp.concatenate(
        [conv_w_term.reshape(-1), head_w_term.reshape(-1), conv_b_term, head_b_term]
    )
    flat = jnp.pad(flat, (0, 40960 - flat.shape[0]))
    summed = total(flat.reshape(32, 10, 128)).reshape(-1)
    conv_w_sum = summed[:36864].reshape(conv_w_term.shape)
    head_w_sum = summed[36864:40832].reshape(head_w_term.shape)
    conv_b_sum = summed[40832:40896]
    head_b_sum = summed[40896:40958]
    slope = jnp.where(x32 > 0.0, jnp.float32(1.0), jnp.exp(jnp.minimum(x32, 0.0)))
    grad_input = (grad_mixed + slope * grad_act).astype(jnp.bfloat16)
    return (
        grad_input,
        conv_w_sum / count,
        conv_b_sum / count,
        head_w_sum / count,
        head_b_sum / count,
    )


def solution(mesh):
    return jax.shard_map(
        per_device,
        mesh=mesh,
        in_specs=(P(None, "col", "row"), P(), P(), P(), P(), P("col", "row"), P("col", "row"), P()),
        out_specs=(P(None, "col", "row"), P(), P(), P(), P()),
        check_vma=False,
    )
```

```python
import functools

import jax
import jax.numpy as jnp
from jax import lax
from jax.experimental import pallas as pl
from jax.experimental.pallas import tpu as pltpu
from jax.sharding import PartitionSpec as P

MESH = pl.DeviceIdType.MESH
F32 = jnp.float32
BF16 = jnp.bfloat16
DB = 37
NB = 62

RIMS = (
    (0, 1, "own", 64, 16, "own", 0),
    (0, -1, "own", 16, 16, "own", 80),
    (1, 0, "right", 0, 8, "from_left", 2),
    (-1, 0, "left", 0, 8, "from_right", 2),
    (1, 1, "right", 6, 2, "from_left", 0),
    (1, -1, "right", 0, 2, "from_left", 10),
    (-1, 1, "left", 6, 2, "from_right", 0),
    (-1, -1, "left", 0, 2, "from_right", 10),
)


def device(x, y, z, core):
    return ((z // 4) * 4 + x, (y * 4 + lax.rem(z, 4)) * 2 + core)


class Place:
    def __init__(self):
        self.row = lax.axis_index("row")
        self.col = lax.axis_index("col")
        self.x = lax.rem(self.row, 4)
        self.core = lax.rem(self.col, 2)
        chip = self.col // 2
        self.y = chip // 4
        self.z = 4 * (self.row // 4) + lax.rem(chip, 4)
        self.spot = 4 * self.y + self.x

    def inside(self, row_step, col_step):
        row, col = self.row + row_step, self.col + col_step
        return (row >= 0) & (row < 16) & (col >= 0) & (col < 32)

    def is_me(self, t):
        return (t[0] == self.x) & (t[1] == self.y) & (t[2] == self.z) & (t[3] == self.core)

    def mirror_first(self, k):
        return (lax.rem(k, 4), k // 4, self.z, self.core)

    def mirror_second(self, s, half):
        return (lax.rem(self.z, 4), self.z // 4, s, half)

    def mirror_giver(self, k, core):
        return (lax.rem(k, 4), k // 4, self.spot, core)

    def plane(self, s):
        return (lax.rem(s // 2, 4), s // 8, self.z, lax.rem(s, 2))

    def plane_slot(self):
        return self.spot * 2 + self.core

    def ring(self, z):
        return (self.x, self.y, z, self.core)


def signal(barrier, target):
    pl.semaphore_signal(barrier, inc=1, device_id=target, device_id_type=MESH)


def greet(me, barrier):
    for row_step, col_step in [r[:2] for r in RIMS]:
        @pl.when(me.inside(row_step, col_step))
        def _():
            signal(barrier, (me.row + row_step, me.col + col_step))

    def mirror_partners(s, carry):
        for t in (me.mirror_first(s), me.mirror_giver(s, 0), me.mirror_giver(s, 1)):
            @pl.when(jnp.logical_not(me.is_me(t)))
            def _():
                signal(barrier, device(*t))
        return carry

    lax.fori_loop(0, 16, mirror_partners, 0)

    def plane_partners(t, carry):
        signal(barrier, device(*me.plane(lax.rem(me.plane_slot() + t, 32))))
        return carry

    lax.fori_loop(1, 32, plane_partners, 0)

    def ring_partners(t, carry):
        signal(barrier, device(*me.ring(lax.rem(me.z + t, 16))))
        return carry

    lax.fori_loop(1, 16, ring_partners, 0)


def await_greetings(me, barrier):
    rows = 3 - jnp.where(me.row == 0, 1, 0) - jnp.where(me.row == 15, 1, 0)
    cols = 3 - jnp.where(me.col == 0, 1, 0) - jnp.where(me.col == 31, 1, 0)
    others = 46 + 47 - jnp.where(me.spot == me.z, 1, 0)
    pl.semaphore_wait(barrier, rows * cols - 1 + others)


def rim_copy(me, refs, sems, at):
    row_step, col_step, source, first, many, target, into = RIMS[at]
    return pltpu.make_async_remote_copy(
        src_ref=refs[source].at[pl.ds(first, many)],
        dst_ref=refs[target].at[pl.ds(into, many)],
        send_sem=sems[0].at[at],
        recv_sem=sems[1].at[at],
        device_id=(me.row + row_step, me.col + col_step),
        device_id_type=MESH,
    )


def send_rims(me, refs, sems):
    for at, (row_step, col_step, _, _, many, target, into) in enumerate(RIMS):
        @pl.when(me.inside(row_step, col_step))
        def _():
            rim_copy(me, refs, sems, at).start()

        @pl.when(jnp.logical_not(me.inside(-row_step, -col_step)))
        def _():
            refs[target][into : into + many] = jnp.zeros((many, 64, 128), BF16)


def await_rims(me, refs, sems):
    for at, (row_step, col_step) in enumerate([r[:2] for r in RIMS]):
        @pl.when(me.inside(-row_step, -col_step))
        def _():
            rim_copy(me, refs, sems, at).wait_recv()


def await_sent_rims(me, refs, sems):
    for at, (row_step, col_step) in enumerate([r[:2] for r in RIMS]):
        @pl.when(me.inside(row_step, col_step))
        def _():
            rim_copy(me, refs, sems, at).wait_send()


def lanes():
    return lax.broadcasted_iota(jnp.int32, (64, 128), 1)


def turn(v, by):
    by = by % 128
    return v if by == 0 else pltpu.roll(v, by, 1)


def gather_edges(rows, left, right, at):
    group = lanes() // 16
    low = turn(rows[0], 0)
    high = turn(rows[0], 16)
    for g in range(1, 8):
        low = jnp.where(group == g, turn(rows[g], 16 * g), low)
        high = jnp.where(group == g, turn(rows[g], 16 * (g + 1)), high)
    left[at] = low.astype(BF16)
    right[at] = high.astype(BF16)


def stack_taps(refs, stack):
    lane = lanes()

    def eight(at, carry):
        before = refs["from_left"][at].astype(F32)
        after = refs["from_right"][at].astype(F32)
        for g in range(8):
            e = at * 8 + g
            cells = refs["own"][e]
            c32 = cells.astype(F32)
            lower = jnp.where(lane < 16, turn(before, -16 * g), turn(c32, 16))
            upper = jnp.where(lane >= 112, turn(after, 112 - 16 * g), turn(c32, 112))
            stack[e, 0:64] = lower.astype(BF16)
            stack[e, 64:128] = cells
            stack[e, 128:192] = upper.astype(BF16)
        return carry

    lax.fori_loop(0, 12, eight, 0)


def window(stack, at):
    return jnp.concatenate(
        [
            jnp.concatenate([stack[at * 8 + r + 16 * a] for a in range(3)], axis=0)
            for r in range(8)
        ],
        axis=1,
    )


def rows_of(ref, at):
    return jnp.concatenate([ref[at * 8 + r] for r in range(8)], axis=1)


def strided(i):
    return pl.ds(i, 64, stride=64)


def block(n, at):
    return pl.ds(pl.multiple_of(n * 64 + at * 8, 8), 8)


def kernel(
    feat, cw, cb, wh, hb, dist, omega, mask,
    grad_out, cw_out, cb_out, wh_out, hb_out,
    flat, logit, held, own, left, right, from_left, from_right, stack, mixed,
    gown, gleft, gright, gfrom_left, gfrom_right, grads,
    wc, wf, whp, wht, bias_c, bias_h,
    packed, tmp, placed, sums, rows, src, parts, mine, whole, ring, dst,
    act_send, act_recv, grad_send, grad_recv,
    a_send, a_recv, b_send, b_recv,
    send_1, recv_1, send_2, recv_2, send_3, recv_3,
):
    me = Place()
    barrier = pltpu.get_barrier_semaphore()
    greet(me, barrier)
    act = dict(own=own, left=left, right=right, from_left=from_left, from_right=from_right)
    grd = dict(own=gown, left=gleft, right=gright, from_left=gfrom_left, from_right=gfrom_right)
    act_sems, grad_sems = (act_send, act_recv), (grad_send, grad_recv)

    def widen(c, carry):
        flat[pl.ds(pl.multiple_of(c * 64, 64), 64), :] = feat[c].astype(F32)
        return carry

    lax.fori_loop(0, 64, widen, 0)

    def activate(at, carry):
        rounded = []
        for g in range(8):
            i = at * 8 + g
            v = flat[strided(i), :]
            held[i] = v.astype(BF16)
            cells = jnp.where(v > 0.0, v, jnp.exp(jnp.minimum(v, 0.0)) - 1.0).astype(BF16)
            own[16 + i] = cells
            rounded.append(cells.astype(F32))
        gather_edges(rounded, left, right, at)
        return carry

    lax.fori_loop(0, 8, activate, 0)
    await_greetings(me, barrier)
    send_rims(me, act, act_sems)

    for k in range(9):
        wc[:, 64 * k : 64 * k + 64] = cw[k]
        wf[:, 64 * k : 64 * k + 64] = cw[8 - k].astype(F32).T.astype(BF16)
    whp[...] = jnp.zeros((64, 64), BF16)
    whp[0:NB, :] = wh[...]
    wht[...] = whp[...].astype(F32).T.astype(BF16)
    bias_c[...] = jnp.broadcast_to(cb[...], (128, 64)).T
    bias_h[...] = jnp.zeros((64, 128), F32)
    bias_h[0:NB, :] = jnp.broadcast_to(hb[...], (128, NB)).T

    await_rims(me, act, act_sems)
    stack_taps(act, stack)

    def forward(at, carry):
        pre = jnp.dot(wc[...], window(stack, at), preferred_element_type=F32)
        pre = pre + jnp.concatenate([bias_c[...]] * 8, axis=1)
        mix = (rows_of(held, at).astype(F32) + pre).astype(BF16)
        out = jnp.dot(whp[...], mix, preferred_element_type=F32)
        out = (out + jnp.concatenate([bias_h[...]] * 8, axis=1)).astype(BF16).astype(F32)
        for r in range(8):
            mixed[at * 8 + r] = mix[:, 128 * r : 128 * r + 128]
            logit[strided(at * 8 + r), :] = out[:, 128 * r : 128 * r + 128]
        return carry

    lax.fori_loop(0, 8, forward, 0)

    low = lanes() < 64

    def pack(m, carry):
        one = logit[pl.ds(pl.multiple_of(m * 64, 64), 64), :]
        two = logit[pl.ds(pl.multiple_of(m * 64 + 2048, 64), 64), :]
        packed[0, m] = jnp.where(low, one, turn(two, 64)).astype(BF16)
        packed[1, m] = jnp.where(low, turn(one, 64), two).astype(BF16)
        return carry

    lax.fori_loop(0, 32, pack, 0)

    def piece(k):
        return pl.ds(k * 2, 2)

    def mirror_a(t, carry):
        k = lax.rem(me.spot + t, 16)
        to = me.mirror_first(k)
        for h in range(2):
            @pl.when(me.is_me(to))
            def _():
                pltpu.make_async_copy(
                    packed.at[h, piece(k)], tmp.at[me.spot, h], a_recv.at[me.spot, h]
                ).start()

            @pl.when(jnp.logical_not(me.is_me(to)))
            def _():
                pltpu.make_async_remote_copy(
                    src_ref=packed.at[h, piece(k)], dst_ref=tmp.at[me.spot, h],
                    send_sem=a_send.at[k, h], recv_sem=a_recv.at[me.spot, h],
                    device_id=device(*to), device_id_type=MESH,
                ).start()
        return carry

    lax.fori_loop(0, 16, mirror_a, 0)

    def mirror_b(t, carry):
        s = lax.rem(me.spot + t, 16)
        for h in range(2):
            pltpu.make_async_copy(packed.at[h, piece(0)], tmp.at[s, h], a_recv.at[s, h]).wait()
            to = me.mirror_second(s, h)

            @pl.when(me.is_me(to))
            def _():
                pltpu.make_async_copy(
                    tmp.at[s, h], placed.at[me.core, piece(me.spot)], b_recv.at[me.core, me.spot]
                ).start()

            @pl.when(jnp.logical_not(me.is_me(to)))
            def _():
                pltpu.make_async_remote_copy(
                    src_ref=tmp.at[s, h], dst_ref=placed.at[me.core, piece(me.spot)],
                    send_sem=b_send.at[s, h], recv_sem=b_recv.at[me.core, me.spot],
                    device_id=device(*to), device_id_type=MESH,
                ).start()
        return carry

    lax.fori_loop(0, 16, mirror_b, 0)

    mine_first = mask[pl.ds(me.col // 2, 1), :].astype(F32)
    mine_first = jnp.broadcast_to(mine_first, (128, 128)).T
    first = jnp.where(me.core == 0, mine_first[0:64], mine_first[64:128])
    pair = first * mask[pl.ds(me.row, 1), :].astype(F32)
    count = jnp.sum(mask[...].astype(F32), keepdims=True)

    def arrive(k, carry):
        for c in range(2):
            pltpu.make_async_copy(
                tmp.at[0, 0], placed.at[c, piece(k)], b_recv.at[c, k]
            ).wait()
        for u in range(2):
            m = k * 2 + u
            other = jnp.concatenate([placed[0, m], placed[1, m]], axis=0).astype(F32).T
            one = pl.ds(pl.multiple_of(m * 64, 64), 64)
            two = pl.ds(pl.multiple_of(m * 64 + 2048, 64), 64)
            flat[one, :] = 0.5 * (logit[one, :] + other[0:64])
            flat[two, :] = 0.5 * (logit[two, :] + other[64:128])
        return carry

    lax.fori_loop(0, 16, arrive, 0)
    sums[0] = pair

    def softmaxes(at, carry):
        eight = pl.ds(pl.multiple_of(at * 8, 8), 8)
        weight = sums[0, eight, :]
        for start, stop, label in ((0, DB, dist), (DB, NB, omega)):
            chosen = label[eight, :]
            top = flat[block(start, at), :]
            for n in range(start + 1, stop):
                top = jnp.maximum(top, flat[block(n, at), :])
            below = jnp.zeros((8, 128), F32)
            for n in range(start, stop):
                e = jnp.exp(flat[block(n, at), :] - top)
                flat[block(n, at), :] = e
                below = below + e
            scale = 1.0 / below
            for n in range(start, stop):
                hot = jnp.where(chosen == n - start, 1.0, 0.0)
                flat[block(n, at), :] = weight * (flat[block(n, at), :] * scale - hot)
        for n in range(NB, 64):
            flat[block(n, at), :] = jnp.zeros((8, 128), F32)
        return carry

    lax.fori_loop(0, 8, softmaxes, 0)

    rows[...] = jnp.zeros((64, 640), F32)
    sums[...] = jnp.zeros((2, 64, 128), F32)

    def backward(at, carry):
        per_row = [flat[strided(at * 8 + r), :] for r in range(8)]
        bins = per_row[0]
        for r in range(1, 8):
            bins = bins + per_row[r]
        sums[0] += bins
        grad_logit = jnp.concatenate([v.astype(BF16) for v in per_row], axis=1)
        back = jnp.dot(wht[...], grad_logit, preferred_element_type=F32)
        pieces = [back[:, 128 * r : 128 * r + 128] for r in range(8)]
        total = pieces[0]
        for r in range(1, 8):
            total = total + pieces[r]
        sums[1] += total
        rounded = []
        for r in range(8):
            grads[at * 8 + r] = pieces[r]
            cells = pieces[r].astype(BF16)
            gown[16 + at * 8 + r] = cells
            rounded.append(cells.astype(F32))
        gather_edges(rounded, gleft, gright, at)
        over_pairs = (((1,), (1,)), ((), ()))
        rows[:, 0:576] += lax.dot_general(
            back.astype(BF16), window(stack, at), over_pairs, preferred_element_type=F32
        )
        rows[:, 576:640] += lax.dot_general(
            grad_logit, rows_of(mixed, at), over_pairs, preferred_element_type=F32
        )
        return carry

    lax.fori_loop(0, 8, backward, 0)
    send_rims(me, grd, grad_sems)

    rows[62:63, 576:640] = jnp.sum(sums[1].T, axis=0, keepdims=True)
    rows[63:64, 576:640] = jnp.sum(sums[0].T, axis=0, keepdims=True)
    for t in range(5):
        whole[64 * t : 64 * t + 64, :] = rows[:, 128 * t : 128 * t + 128]
    for s in range(32):
        src[s] = whole[10 * s : 10 * s + 10, :]
    slot = me.plane_slot()

    def send_parts(t, carry):
        s = lax.rem(slot + t, 32)
        pltpu.make_async_remote_copy(
            src_ref=src.at[s], dst_ref=parts.at[slot], send_sem=send_1.at[s],
            recv_sem=recv_1.at[slot], device_id=device(*me.plane(s)), device_id_type=MESH,
        ).start()
        return carry

    lax.fori_loop(1, 32, send_parts, 0)
    parts[slot] = src[slot]

    await_rims(me, grd, grad_sems)
    stack_taps(grd, stack)

    def wait_parts(t, carry):
        s = lax.rem(slot + t, 32)
        pltpu.make_async_copy(src.at[0], parts.at[s], recv_1.at[s]).wait()
        return carry

    lax.fori_loop(1, 32, wait_parts, 0)
    mine[0] = jnp.sum(parts[...], axis=0)
    ring[me.z] = mine[0]

    def send_ring(t, carry):
        o = lax.rem(me.z + t, 16)
        pltpu.make_async_remote_copy(
            src_ref=mine.at[0], dst_ref=ring.at[me.z], send_sem=send_2.at[o],
            recv_sem=recv_2.at[me.z], device_id=device(*me.ring(o)), device_id_type=MESH,
        ).start()
        return carry

    lax.fori_loop(1, 16, send_ring, 0)

    def inputs(at, carry):
        back = jnp.dot(wf[...], window(stack, at), preferred_element_type=F32)
        for r in range(8):
            i = at * 8 + r
            v = held[i].astype(F32)
            slope = jnp.where(v > 0.0, 1.0, jnp.exp(jnp.minimum(v, 0.0)))
            flat[strided(i), :] = grads[i] + slope * back[:, 128 * r : 128 * r + 128]
        return carry

    lax.fori_loop(0, 8, inputs, 0)

    def wait_ring(t, carry):
        o = lax.rem(me.z + t, 16)
        pltpu.make_async_copy(mine.at[0], ring.at[o], recv_2.at[o]).wait()
        return carry

    lax.fori_loop(1, 16, wait_ring, 0)
    mine[1] = jnp.sum(ring[...], axis=0)
    dst[slot] = mine[1]

    def send_all(t, carry):
        s = lax.rem(slot + t, 32)
        pltpu.make_async_remote_copy(
            src_ref=mine.at[1], dst_ref=dst.at[slot], send_sem=send_3.at[s],
            recv_sem=recv_3.at[slot], device_id=device(*me.plane(s)), device_id_type=MESH,
        ).start()
        return carry

    lax.fori_loop(1, 32, send_all, 0)

    def narrow(c, carry):
        grad_out[c] = flat[pl.ds(pl.multiple_of(c * 64, 64), 64), :].astype(BF16)
        return carry

    lax.fori_loop(0, 64, narrow, 0)

    def wait_all(t, carry):
        s = lax.rem(slot + t, 32)
        pltpu.make_async_copy(mine.at[1], dst.at[s], recv_3.at[s]).wait()
        return carry

    lax.fori_loop(1, 32, wait_all, 0)
    for s in range(32):
        whole[10 * s : 10 * s + 10, :] = dst[s]
    for k in range(9):
        t, half = k // 2, k % 2
        cw_out[k] = whole[64 * t : 64 * t + 64, 64 * half : 64 * half + 64] / count
    wh_out[...] = whole[256 : 256 + NB, 64:128] / count
    cb_out[...] = whole[318:319, 64:128] / count
    hb_out[...] = whole[319:320, 64 : 64 + NB] / count

    await_sent_rims(me, act, act_sems)
    await_sent_rims(me, grd, grad_sems)

    def sent_mirror(k, carry):
        for h in range(2):
            @pl.when(jnp.logical_not(me.is_me(me.mirror_first(k))))
            def _():
                pltpu.make_async_copy(packed.at[h, piece(k)], tmp.at[0, h], a_send.at[k, h]).wait()

            @pl.when(jnp.logical_not(me.is_me(me.mirror_second(k, h))))
            def _():
                pltpu.make_async_copy(tmp.at[k, h], placed.at[0, piece(0)], b_send.at[k, h]).wait()
        return carry

    lax.fori_loop(0, 16, sent_mirror, 0)

    def sent_plane(t, carry):
        s = lax.rem(slot + t, 32)
        pltpu.make_async_copy(mine.at[0], dst.at[s], send_1.at[s]).wait()
        pltpu.make_async_copy(mine.at[0], dst.at[s], send_3.at[s]).wait()
        return carry

    lax.fori_loop(1, 32, sent_plane, 0)

    def sent_ring(t, carry):
        o = lax.rem(me.z + t, 16)
        pltpu.make_async_copy(mine.at[0], ring.at[o], send_2.at[o]).wait()
        return carry

    lax.fori_loop(1, 16, sent_ring, 0)


def per_device(
    features, conv_weight, conv_bias, head_weight, head_bias, dist_label, omega_label, residue_mask
):
    vmem = pl.BlockSpec(memory_space=pltpu.VMEM)
    cells = (64, 128)
    dma = pltpu.SemaphoreType.DMA
    scratch = [
        pltpu.VMEM((4096, 128), F32),
        pltpu.VMEM((4096, 128), F32),
        pltpu.VMEM((64,) + cells, BF16),
        pltpu.VMEM((96,) + cells, BF16),
        pltpu.VMEM((8,) + cells, BF16),
        pltpu.VMEM((8,) + cells, BF16),
        pltpu.VMEM((12,) + cells, BF16),
        pltpu.VMEM((12,) + cells, BF16),
        pltpu.VMEM((96, 192, 128), BF16),
        pltpu.VMEM((64,) + cells, BF16),
        pltpu.VMEM((96,) + cells, BF16),
        pltpu.VMEM((8,) + cells, BF16),
        pltpu.VMEM((8,) + cells, BF16),
        pltpu.VMEM((12,) + cells, BF16),
        pltpu.VMEM((12,) + cells, BF16),
        pltpu.VMEM((64,) + cells, F32),
        pltpu.VMEM((64, 576), BF16),
        pltpu.VMEM((64, 576), BF16),
        pltpu.VMEM((64, 64), BF16),
        pltpu.VMEM((64, 64), BF16),
        pltpu.VMEM(cells, F32),
        pltpu.VMEM(cells, F32),
        pltpu.VMEM((2, 32) + cells, BF16),
        pltpu.VMEM((16, 2, 2) + cells, BF16),
        pltpu.VMEM((2, 32) + cells, BF16),
        pltpu.VMEM((2,) + cells, F32),
        pltpu.VMEM((64, 640), F32),
        pltpu.VMEM((32, 10, 128), F32),
        pltpu.VMEM((32, 10, 128), F32),
        pltpu.VMEM((2, 10, 128), F32),
        pltpu.VMEM((320, 128), F32),
        pltpu.VMEM((16, 10, 128), F32),
        pltpu.VMEM((32, 10, 128), F32),
        dma((8,)), dma((8,)), dma((8,)), dma((8,)),
        dma((16, 2)), dma((16, 2)), dma((16, 2)), dma((2, 16)),
        dma((32,)), dma((32,)), dma((16,)), dma((16,)), dma((32,)), dma((32,)),
    ]
    grad_input, conv_w, conv_b, head_w, head_b = pl.pallas_call(
        kernel,
        out_shape=(
            jax.ShapeDtypeStruct(features.shape, BF16),
            jax.ShapeDtypeStruct((9, 64, 64), F32),
            jax.ShapeDtypeStruct((1, 64), F32),
            jax.ShapeDtypeStruct((NB, 64), F32),
            jax.ShapeDtypeStruct((1, NB), F32),
        ),
        in_specs=[vmem] * 8,
        out_specs=(vmem,) * 5,
        scratch_shapes=scratch,
        compiler_params=pltpu.CompilerParams(collective_id=1, has_side_effects=True),
        name="pair_head",
    )(
        features,
        conv_weight.reshape(9, 64, 64),
        conv_bias.reshape(1, 64),
        head_weight,
        head_bias.reshape(1, NB),
        dist_label,
        omega_label,
        residue_mask.reshape(16, 128),
    )
    return (
        grad_input,
        conv_w.reshape(3, 3, 64, 64),
        conv_b.reshape(64),
        head_w,
        head_b.reshape(NB),
    )


def solution(mesh):
    return jax.shard_map(
        per_device,
        mesh=mesh,
        in_specs=(P(None, "col", "row"), P(), P(), P(), P(), P("col", "row"), P("col", "row"), P()),
        out_specs=(P(None, "col", "row"), P(), P(), P(), P()),
        check_vma=False,
    )
```

```python
import functools

import jax
import jax.numpy as jnp
from jax import lax
from jax.experimental import pallas as pl
from jax.experimental.pallas import tpu as pltpu
from jax.sharding import PartitionSpec as P

MESH = pl.DeviceIdType.MESH
F32 = jnp.float32
BF16 = jnp.bfloat16
DB = 37
NB = 62
RIM_SEMS = (
    "band_send", "band_recv", "edge_send", "edge_recv", "via_send", "via_recv",
    "relay_send", "corner_send", "corner_recv",
)

def device(x, y, z, core):
    return ((z // 4) * 4 + x, (y * 4 + lax.rem(z, 4)) * 2 + core)


class Place:
    def __init__(self):
        self.row = lax.axis_index("row")
        self.col = lax.axis_index("col")
        self.x = lax.rem(self.row, 4)
        self.core = lax.rem(self.col, 2)
        chip = self.col // 2
        self.y = chip // 4
        self.block = self.row // 4
        self.z = 4 * self.block + lax.rem(chip, 4)
        self.spot = 4 * self.y + self.x

    def is_me(self, t):
        return (t[0] == self.x) & (t[1] == self.y) & (t[2] == self.z) & (t[3] == self.core)

    def mirror_first(self, k):
        return (lax.rem(k, 4), k // 4, self.z, self.core)

    def mirror_second(self, s, half):
        return (lax.rem(self.z, 4), self.z // 4, s, half)

    def mirror_giver(self, k, core):
        return (lax.rem(k, 4), k // 4, self.spot, core)

    def plane(self, s):
        return (lax.rem(s // 2, 4), s // 8, self.z, lax.rem(s, 2))

    def plane_slot(self):
        return self.spot * 2 + self.core

    def ring(self, z):
        return (self.x, self.y, z, self.core)


def signal(barrier, target):
    pl.semaphore_signal(barrier, inc=1, device_id=target, device_id_type=MESH)


def next_along_row(me, flow):
    return (me.row + 1, me.col) if flow == 0 else (me.row - 1, me.col)


def near(me, flow):
    return me.x < 3 if flow == 0 else me.x > 0


def far_open(me, flow):
    return me.block < 3 if flow == 0 else me.block > 0


def far_source(flow):
    return 3 if flow == 0 else 0


def far_target(me, flow):
    if flow == 0:
        return device(0, me.y, me.z + 4, me.core)
    return device(3, me.y, me.z - 4, me.core)


def receives(me, flow):
    return me.row > 0 if flow == 0 else me.row < 15


def col_open(me, side):
    return me.col > 0 if side == 0 else me.col < 31


def next_along_col(me, side):
    return (me.row, me.col - 1) if side == 0 else (me.row, me.col + 1)


def greet(me, barrier):
    for side in range(2):
        @pl.when(col_open(me, side))
        def _():
            signal(barrier, next_along_col(me, side))

    for flow in range(2):
        @pl.when(near(me, flow))
        def _():
            signal(barrier, next_along_row(me, flow))

    def far_partners(k, carry):
        @pl.when((me.x == 0) & (me.block > 0))
        def _():
            signal(barrier, device(k, me.y, me.z - 4, me.core))

        @pl.when((me.x == 3) & (me.block < 3))
        def _():
            signal(barrier, device(k, me.y, me.z + 4, me.core))
        return carry

    lax.fori_loop(0, 4, far_partners, 0)

    def mirror_partners(s, carry):
        for t in (me.mirror_first(s), me.mirror_giver(s, 0), me.mirror_giver(s, 1)):
            @pl.when(jnp.logical_not(me.is_me(t)))
            def _():
                signal(barrier, device(*t))
        return carry

    lax.fori_loop(0, 16, mirror_partners, 0)

    def plane_partners(t, carry):
        signal(barrier, device(*me.plane(lax.rem(me.plane_slot() + t, 32))))
        return carry

    lax.fori_loop(1, 32, plane_partners, 0)

    def ring_partners(t, carry):
        signal(barrier, device(*me.ring(lax.rem(me.z + t, 16))))
        return carry

    lax.fori_loop(1, 16, ring_partners, 0)


def await_greetings(me, barrier):
    total = 46 + 47 - jnp.where(me.spot == me.z, 1, 0)
    for k in range(2):
        for known in (col_open(me, k), near(me, k), far_open(me, k)):
            total = total + jnp.where(known, 1, 0)
    pl.semaphore_wait(barrier, total)


def remote(source, target, sent, arrived, to):
    return pltpu.make_async_remote_copy(
        src_ref=source, dst_ref=target, send_sem=sent, recv_sem=arrived,
        device_id=to, device_id_type=MESH,
    )


def edge(refs, flow, k):
    return refs[("right", "left")[flow]].at[pl.ds(2 * k, 2)]


def rim(refs, flow, k):
    return refs[("from_left", "from_right")[flow]].at[pl.ds(2 * k + 2, 2)]


def band_copy(me, refs, sems, side):
    first, into = ((16, 80), (64, 0))[side]
    return remote(
        refs["own"].at[pl.ds(first, 16)], refs["own"].at[pl.ds(into, 16)],
        sems["band_send"].at[side], sems["band_recv"].at[side], next_along_col(me, side),
    )


def edge_copy(me, refs, sems, flow, k, to):
    return remote(
        edge(refs, flow, k), rim(refs, flow, k),
        sems["edge_send"].at[flow, k], sems["edge_recv"].at[flow, k], to,
    )


def via_copy(me, refs, sems, flow, k):
    return remote(
        edge(refs, flow, k), refs["via"].at[flow],
        sems["via_send"].at[flow, k], sems["via_recv"].at[flow],
        device(k, me.y, me.z, me.core),
    )


def relay_copy(me, refs, sems, flow):
    return remote(
        refs["via"].at[flow], rim(refs, flow, me.x),
        sems["relay_send"].at[flow], sems["edge_recv"].at[flow, me.x], far_target(me, flow),
    )


def corner_copy(me, refs, sems, flow, side):
    held = refs[("from_left", "from_right")[flow]]
    first, into = ((2, 10), (8, 0))[side]
    return remote(
        held.at[pl.ds(first, 2)], held.at[pl.ds(into, 2)],
        sems["corner_send"].at[flow, side], sems["corner_recv"].at[flow, side],
        next_along_col(me, side),
    )


def send_rims(me, refs, sems):
    for flow in range(2):
        own = far_source(flow)

        @pl.when((me.x == own) & far_open(me, flow))
        def _():
            for k in range(4):
                if k != own:
                    via_copy(me, refs, sems, flow, k).start()
            edge_copy(me, refs, sems, flow, own, far_target(me, flow)).start()

        @pl.when(near(me, flow))
        def _():
            for k in range(4):
                edge_copy(me, refs, sems, flow, k, next_along_row(me, flow)).start()

    for side in range(2):
        @pl.when(col_open(me, side))
        def _():
            band_copy(me, refs, sems, side).start()

        @pl.when(jnp.logical_not(col_open(me, side)))
        def _():
            into = (0, 80)[side]
            refs["own"][into : into + 16] = jnp.zeros((16, 64, 128), BF16)
            into = (0, 10)[side]
            refs["from_left"][into : into + 2] = jnp.zeros((2, 64, 128), BF16)
            refs["from_right"][into : into + 2] = jnp.zeros((2, 64, 128), BF16)

    for flow in range(2):
        @pl.when(jnp.logical_not(receives(me, flow)))
        def _():
            refs[("from_left", "from_right")[flow]][...] = jnp.zeros((12, 64, 128), BF16)


def relay_rims(me, refs, sems):
    for flow in range(2):
        @pl.when((me.x != far_source(flow)) & far_open(me, flow))
        def _():
            via_copy(me, refs, sems, flow, 0).wait_recv()
            relay_copy(me, refs, sems, flow).start()


def await_rims(me, refs, sems):
    for flow in range(2):
        for k in (0, 3, 1, 2):
            @pl.when(receives(me, flow))
            def _():
                edge_copy(me, refs, sems, flow, k, next_along_row(me, flow)).wait_recv()

            if k in (0, 3):
                side = k // 3

                @pl.when(receives(me, flow) & col_open(me, side))
                def _():
                    corner_copy(me, refs, sems, flow, side).start()

    for side in range(2):
        @pl.when(col_open(me, 1 - side))
        def _():
            band_copy(me, refs, sems, side).wait_recv()

        for flow in range(2):
            @pl.when(receives(me, flow) & col_open(me, 1 - side))
            def _():
                corner_copy(me, refs, sems, flow, side).wait_recv()


def await_sent_rims(me, refs, sems):
    for flow in range(2):
        own = far_source(flow)

        @pl.when((me.x == own) & far_open(me, flow))
        def _():
            for k in range(4):
                if k != own:
                    via_copy(me, refs, sems, flow, k).wait_send()
            edge_copy(me, refs, sems, flow, own, far_target(me, flow)).wait_send()

        @pl.when((me.x != own) & far_open(me, flow))
        def _():
            relay_copy(me, refs, sems, flow).wait_send()

        @pl.when(near(me, flow))
        def _():
            for k in range(4):
                edge_copy(me, refs, sems, flow, k, next_along_row(me, flow)).wait_send()

        for side in range(2):
            @pl.when(receives(me, flow) & col_open(me, side))
            def _():
                corner_copy(me, refs, sems, flow, side).wait_send()

    for side in range(2):
        @pl.when(col_open(me, side))
        def _():
            band_copy(me, refs, sems, side).wait_send()


def lanes():
    return lax.broadcasted_iota(jnp.int32, (64, 128), 1)


def turn(v, by):
    by = by % 128
    return v if by == 0 else pltpu.roll(v, by, 1)


def gather_edges(rows, left, right, at):
    group = lanes() // 16
    low = turn(rows[0], 0)
    high = turn(rows[0], 16)
    for g in range(1, 8):
        low = jnp.where(group == g, turn(rows[g], 16 * g), low)
        high = jnp.where(group == g, turn(rows[g], 16 * (g + 1)), high)
    left[at] = low.astype(BF16)
    right[at] = high.astype(BF16)


def stack_taps(refs, stack):
    lane = lanes()

    def eight(at, carry):
        before = refs["from_left"][at].astype(F32)
        after = refs["from_right"][at].astype(F32)
        for g in range(8):
            e = at * 8 + g
            cells = refs["own"][e]
            c32 = cells.astype(F32)
            lower = jnp.where(lane < 16, turn(before, -16 * g), turn(c32, 16))
            upper = jnp.where(lane >= 112, turn(after, 112 - 16 * g), turn(c32, 112))
            stack[e, 0:64] = lower.astype(BF16)
            stack[e, 64:128] = cells
            stack[e, 128:192] = upper.astype(BF16)
        return carry

    lax.fori_loop(0, 12, eight, 0)


def window(stack, at):
    return jnp.concatenate(
        [
            jnp.concatenate([stack[at * 8 + r + 16 * a] for a in range(3)], axis=0)
            for r in range(8)
        ],
        axis=1,
    )


def rows_of(ref, at):
    return jnp.concatenate([ref[at * 8 + r] for r in range(8)], axis=1)


def strided(i):
    return pl.ds(i, 64, stride=64)


def block(n, at):
    return pl.ds(pl.multiple_of(n * 64 + at * 8, 8), 8)


def kernel(
    feat, cw, cb, wh, hb, dist, omega, mask,
    grad_out, cw_out, cb_out, wh_out, hb_out,
    flat, logit, held, own, left, right, from_left, from_right, via, stack, mixed,
    gown, gleft, gright, gfrom_left, gfrom_right, gvia, grads,
    wc, wf, whp, wht, bias_c, bias_h,
    packed, tmp, placed, sums, rows, src, parts, mine, whole, ring, dst,
    a_send, a_recv, b_send, b_recv,
    send_1, recv_1, send_2, recv_2, send_3, recv_3,
    *rim_sems,
):
    act_sems = dict(zip(RIM_SEMS, rim_sems[:9]))
    grad_sems = dict(zip(RIM_SEMS, rim_sems[9:]))
    me = Place()
    barrier = pltpu.get_barrier_semaphore()
    greet(me, barrier)
    act = dict(own=own, left=left, right=right, from_left=from_left, from_right=from_right, via=via)
    grd = dict(own=gown, left=gleft, right=gright, from_left=gfrom_left, from_right=gfrom_right, via=gvia)

    def widen(c, carry):
        flat[pl.ds(pl.multiple_of(c * 64, 64), 64), :] = feat[c].astype(F32)
        return carry

    lax.fori_loop(0, 64, widen, 0)

    def activate(at, carry):
        rounded = []
        for g in range(8):
            i = at * 8 + g
            v = flat[strided(i), :]
            held[i] = v.astype(BF16)
            cells = jnp.where(v > 0.0, v, jnp.exp(jnp.minimum(v, 0.0)) - 1.0).astype(BF16)
            own[16 + i] = cells
            rounded.append(cells.astype(F32))
        gather_edges(rounded, left, right, at)
        return carry

    lax.fori_loop(0, 8, activate, 0)
    await_greetings(me, barrier)
    send_rims(me, act, act_sems)

    relay_rims(me, act, act_sems)

    for k in range(9):
        wc[:, 64 * k : 64 * k + 64] = cw[k]
        wf[:, 64 * k : 64 * k + 64] = cw[8 - k].astype(F32).T.astype(BF16)
    whp[...] = jnp.zeros((64, 64), BF16)
    whp[0:NB, :] = wh[...]
    wht[...] = whp[...].astype(F32).T.astype(BF16)
    bias_c[...] = jnp.broadcast_to(cb[...], (128, 64)).T
    bias_h[...] = jnp.zeros((64, 128), F32)
    bias_h[0:NB, :] = jnp.broadcast_to(hb[...], (128, NB)).T

    await_rims(me, act, act_sems)
    stack_taps(act, stack)

    def forward(at, carry):
        pre = jnp.dot(wc[...], window(stack, at), preferred_element_type=F32)
        pre = pre + jnp.concatenate([bias_c[...]] * 8, axis=1)
        mix = (rows_of(held, at).astype(F32) + pre).astype(BF16)
        out = jnp.dot(whp[...], mix, preferred_element_type=F32)
        out = (out + jnp.concatenate([bias_h[...]] * 8, axis=1)).astype(BF16).astype(F32)
        for r in range(8):
            mixed[at * 8 + r] = mix[:, 128 * r : 128 * r + 128]
            logit[strided(at * 8 + r), :] = out[:, 128 * r : 128 * r + 128]
        return carry

    lax.fori_loop(0, 8, forward, 0)

    low = lanes() < 64

    def pack(m, carry):
        one = logit[pl.ds(pl.multiple_of(m * 64, 64), 64), :]
        two = logit[pl.ds(pl.multiple_of(m * 64 + 2048, 64), 64), :]
        packed[0, m] = jnp.where(low, one, turn(two, 64)).astype(BF16)
        packed[1, m] = jnp.where(low, turn(one, 64), two).astype(BF16)
        return carry

    lax.fori_loop(0, 32, pack, 0)

    def piece(k):
        return pl.ds(k * 2, 2)

    apart = lax.rem(me.spot - me.z + 16, 16)
    apart = lax.rem(jnp.minimum(apart, 16 - apart), 8)

    def mirror_a(t, carry):
        k = lax.rem(apart - t // 2 + 8, 8) + 8 * lax.rem(t, 2)
        to = me.mirror_first(k)
        for h in range(2):
            @pl.when(me.is_me(to))
            def _():
                pltpu.make_async_copy(
                    packed.at[h, piece(k)], tmp.at[me.spot, h], a_recv.at[me.spot, h]
                ).start()

            @pl.when(jnp.logical_not(me.is_me(to)))
            def _():
                pltpu.make_async_remote_copy(
                    src_ref=packed.at[h, piece(k)], dst_ref=tmp.at[me.spot, h],
                    send_sem=a_send.at[k, h], recv_sem=a_recv.at[me.spot, h],
                    device_id=device(*to), device_id_type=MESH,
                ).start()
        return carry

    lax.fori_loop(0, 16, mirror_a, 0)

    def mirror_b(t, carry):
        p = lax.rem(me.spot + t // 2, 8)
        back = jnp.where(p == 0, 8, 16 - p)
        s = lax.rem(me.z + jnp.where(lax.rem(t, 2) == 0, p, back), 16)
        for h in range(2):
            pltpu.make_async_copy(packed.at[h, piece(0)], tmp.at[s, h], a_recv.at[s, h]).wait()
            to = me.mirror_second(s, h)

            @pl.when(me.is_me(to))
            def _():
                pltpu.make_async_copy(
                    tmp.at[s, h], placed.at[me.core, piece(me.spot)], b_recv.at[me.core, me.spot]
                ).start()

            @pl.when(jnp.logical_not(me.is_me(to)))
            def _():
                pltpu.make_async_remote_copy(
                    src_ref=tmp.at[s, h], dst_ref=placed.at[me.core, piece(me.spot)],
                    send_sem=b_send.at[s, h], recv_sem=b_recv.at[me.core, me.spot],
                    device_id=device(*to), device_id_type=MESH,
                ).start()
        return carry

    lax.fori_loop(0, 16, mirror_b, 0)

    mine_first = mask[pl.ds(me.col // 2, 1), :].astype(F32)
    mine_first = jnp.broadcast_to(mine_first, (128, 128)).T
    first = jnp.where(me.core == 0, mine_first[0:64], mine_first[64:128])
    pair = first * mask[pl.ds(me.row, 1), :].astype(F32)
    count = jnp.sum(mask[...].astype(F32), keepdims=True)

    def arrive(k, carry):
        for c in range(2):
            pltpu.make_async_copy(
                tmp.at[0, 0], placed.at[c, piece(k)], b_recv.at[c, k]
            ).wait()
        for u in range(2):
            m = k * 2 + u
            other = jnp.concatenate([placed[0, m], placed[1, m]], axis=0).astype(F32).T
            one = pl.ds(pl.multiple_of(m * 64, 64), 64)
            two = pl.ds(pl.multiple_of(m * 64 + 2048, 64), 64)
            flat[one, :] = 0.5 * (logit[one, :] + other[0:64])
            flat[two, :] = 0.5 * (logit[two, :] + other[64:128])
        return carry

    lax.fori_loop(0, 16, arrive, 0)
    sums[0] = pair

    def softmaxes(at, carry):
        eight = pl.ds(pl.multiple_of(at * 8, 8), 8)
        weight = sums[0, eight, :]
        for start, stop, label in ((0, DB, dist), (DB, NB, omega)):
            chosen = label[eight, :]
            top = flat[block(start, at), :]
            for n in range(start + 1, stop):
                top = jnp.maximum(top, flat[block(n, at), :])
            below = jnp.zeros((8, 128), F32)
            for n in range(start, stop):
                e = jnp.exp(flat[block(n, at), :] - top)
                flat[block(n, at), :] = e
                below = below + e
            scale = 1.0 / below
            for n in range(start, stop):
                hot = jnp.where(chosen == n - start, 1.0, 0.0)
                flat[block(n, at), :] = weight * (flat[block(n, at), :] * scale - hot)
        for n in range(NB, 64):
            flat[block(n, at), :] = jnp.zeros((8, 128), F32)
        return carry

    lax.fori_loop(0, 8, softmaxes, 0)

    rows[...] = jnp.zeros((64, 640), F32)
    sums[...] = jnp.zeros((2, 64, 128), F32)

    def backward(at, carry):
        per_row = [flat[strided(at * 8 + r), :] for r in range(8)]
        bins = per_row[0]
        for r in range(1, 8):
            bins = bins + per_row[r]
        sums[0] += bins
        grad_logit = jnp.concatenate([v.astype(BF16) for v in per_row], axis=1)
        back = jnp.dot(wht[...], grad_logit, preferred_element_type=F32)
        pieces = [back[:, 128 * r : 128 * r + 128] for r in range(8)]
        total = pieces[0]
        for r in range(1, 8):
            total = total + pieces[r]
        sums[1] += total
        rounded = []
        for r in range(8):
            grads[at * 8 + r] = pieces[r]
            cells = pieces[r].astype(BF16)
            gown[16 + at * 8 + r] = cells
            rounded.append(cells.astype(F32))
        gather_edges(rounded, gleft, gright, at)
        over_pairs = (((1,), (1,)), ((), ()))
        rows[:, 0:576] += lax.dot_general(
            back.astype(BF16), window(stack, at), over_pairs, preferred_element_type=F32
        )
        rows[:, 576:640] += lax.dot_general(
            grad_logit, rows_of(mixed, at), over_pairs, preferred_element_type=F32
        )
        return carry

    lax.fori_loop(0, 8, backward, 0)
    send_rims(me, grd, grad_sems)

    rows[62:63, 576:640] = jnp.sum(sums[1].T, axis=0, keepdims=True)
    rows[63:64, 576:640] = jnp.sum(sums[0].T, axis=0, keepdims=True)
    for t in range(5):
        whole[64 * t : 64 * t + 64, :] = rows[:, 128 * t : 128 * t + 128]
    for s in range(32):
        src[s] = whole[10 * s : 10 * s + 10, :]
    slot = me.plane_slot()

    def send_parts(t, carry):
        s = lax.rem(slot + t, 32)
        pltpu.make_async_remote_copy(
            src_ref=src.at[s], dst_ref=parts.at[slot], send_sem=send_1.at[s],
            recv_sem=recv_1.at[slot], device_id=device(*me.plane(s)), device_id_type=MESH,
        ).start()
        return carry

    lax.fori_loop(1, 32, send_parts, 0)
    parts[slot] = src[slot]

    relay_rims(me, grd, grad_sems)

    def wait_parts(t, carry):
        s = lax.rem(slot + t, 32)
        pltpu.make_async_copy(src.at[0], parts.at[s], recv_1.at[s]).wait()
        return carry

    lax.fori_loop(1, 32, wait_parts, 0)
    mine[0] = jnp.sum(parts[...], axis=0)
    ring[me.z] = mine[0]

    def send_ring(t, carry):
        o = lax.rem(me.z + t, 16)
        pltpu.make_async_remote_copy(
            src_ref=mine.at[0], dst_ref=ring.at[me.z], send_sem=send_2.at[o],
            recv_sem=recv_2.at[me.z], device_id=device(*me.ring(o)), device_id_type=MESH,
        ).start()
        return carry

    lax.fori_loop(1, 16, send_ring, 0)

    await_rims(me, grd, grad_sems)
    stack_taps(grd, stack)

    def inputs(at, carry):
        back = jnp.dot(wf[...], window(stack, at), preferred_element_type=F32)
        for r in range(8):
            i = at * 8 + r
            v = held[i].astype(F32)
            slope = jnp.where(v > 0.0, 1.0, jnp.exp(jnp.minimum(v, 0.0)))
            flat[strided(i), :] = grads[i] + slope * back[:, 128 * r : 128 * r + 128]
        return carry

    lax.fori_loop(0, 8, inputs, 0)

    def wait_ring(t, carry):
        o = lax.rem(me.z + t, 16)
        pltpu.make_async_copy(mine.at[0], ring.at[o], recv_2.at[o]).wait()
        return carry

    lax.fori_loop(1, 16, wait_ring, 0)
    mine[1] = jnp.sum(ring[...], axis=0)
    dst[slot] = mine[1]

    def send_all(t, carry):
        s = lax.rem(slot + t, 32)
        pltpu.make_async_remote_copy(
            src_ref=mine.at[1], dst_ref=dst.at[slot], send_sem=send_3.at[s],
            recv_sem=recv_3.at[slot], device_id=device(*me.plane(s)), device_id_type=MESH,
        ).start()
        return carry

    lax.fori_loop(1, 32, send_all, 0)

    def narrow(c, carry):
        grad_out[c] = flat[pl.ds(pl.multiple_of(c * 64, 64), 64), :].astype(BF16)
        return carry

    lax.fori_loop(0, 64, narrow, 0)

    def wait_all(t, carry):
        s = lax.rem(slot + t, 32)
        pltpu.make_async_copy(mine.at[1], dst.at[s], recv_3.at[s]).wait()
        return carry

    lax.fori_loop(1, 32, wait_all, 0)
    for s in range(32):
        whole[10 * s : 10 * s + 10, :] = dst[s]
    for k in range(9):
        t, half = k // 2, k % 2
        cw_out[k] = whole[64 * t : 64 * t + 64, 64 * half : 64 * half + 64] / count
    wh_out[...] = whole[256 : 256 + NB, 64:128] / count
    cb_out[...] = whole[318:319, 64:128] / count
    hb_out[...] = whole[319:320, 64 : 64 + NB] / count

    await_sent_rims(me, act, act_sems)
    await_sent_rims(me, grd, grad_sems)

    def sent_mirror(k, carry):
        for h in range(2):
            @pl.when(jnp.logical_not(me.is_me(me.mirror_first(k))))
            def _():
                pltpu.make_async_copy(packed.at[h, piece(k)], tmp.at[0, h], a_send.at[k, h]).wait()

            @pl.when(jnp.logical_not(me.is_me(me.mirror_second(k, h))))
            def _():
                pltpu.make_async_copy(tmp.at[k, h], placed.at[0, piece(0)], b_send.at[k, h]).wait()
        return carry

    lax.fori_loop(0, 16, sent_mirror, 0)

    def sent_plane(t, carry):
        s = lax.rem(slot + t, 32)
        pltpu.make_async_copy(mine.at[0], dst.at[s], send_1.at[s]).wait()
        pltpu.make_async_copy(mine.at[0], dst.at[s], send_3.at[s]).wait()
        return carry

    lax.fori_loop(1, 32, sent_plane, 0)

    def sent_ring(t, carry):
        o = lax.rem(me.z + t, 16)
        pltpu.make_async_copy(mine.at[0], ring.at[o], send_2.at[o]).wait()
        return carry

    lax.fori_loop(1, 16, sent_ring, 0)


def per_device(
    features, conv_weight, conv_bias, head_weight, head_bias, dist_label, omega_label, residue_mask
):
    vmem = pl.BlockSpec(memory_space=pltpu.VMEM)
    cells = (64, 128)
    dma = pltpu.SemaphoreType.DMA
    scratch = [
        pltpu.VMEM((4096, 128), F32),
        pltpu.VMEM((4096, 128), F32),
        pltpu.VMEM((64,) + cells, BF16),
        pltpu.VMEM((96,) + cells, BF16),
        pltpu.VMEM((8,) + cells, BF16),
        pltpu.VMEM((8,) + cells, BF16),
        pltpu.VMEM((12,) + cells, BF16),
        pltpu.VMEM((12,) + cells, BF16),
        pltpu.VMEM((2, 2) + cells, BF16),
        pltpu.VMEM((96, 192, 128), BF16),
        pltpu.VMEM((64,) + cells, BF16),
        pltpu.VMEM((96,) + cells, BF16),
        pltpu.VMEM((8,) + cells, BF16),
        pltpu.VMEM((8,) + cells, BF16),
        pltpu.VMEM((12,) + cells, BF16),
        pltpu.VMEM((12,) + cells, BF16),
        pltpu.VMEM((2, 2) + cells, BF16),
        pltpu.VMEM((64,) + cells, F32),
        pltpu.VMEM((64, 576), BF16),
        pltpu.VMEM((64, 576), BF16),
        pltpu.VMEM((64, 64), BF16),
        pltpu.VMEM((64, 64), BF16),
        pltpu.VMEM(cells, F32),
        pltpu.VMEM(cells, F32),
        pltpu.VMEM((2, 32) + cells, BF16),
        pltpu.VMEM((16, 2, 2) + cells, BF16),
        pltpu.VMEM((2, 32) + cells, BF16),
        pltpu.VMEM((2,) + cells, F32),
        pltpu.VMEM((64, 640), F32),
        pltpu.VMEM((32, 10, 128), F32),
        pltpu.VMEM((32, 10, 128), F32),
        pltpu.VMEM((2, 10, 128), F32),
        pltpu.VMEM((320, 128), F32),
        pltpu.VMEM((16, 10, 128), F32),
        pltpu.VMEM((32, 10, 128), F32),
        dma((16, 2)), dma((16, 2)), dma((16, 2)), dma((2, 16)),
        dma((32,)), dma((32,)), dma((16,)), dma((16,)), dma((32,)), dma((32,)),
    ] + 2 * [
        dma((2,)), dma((2,)), dma((2, 4)), dma((2, 4)), dma((2, 4)), dma((2,)),
        dma((2,)), dma((2, 2)), dma((2, 2)),
    ]
    grad_input, conv_w, conv_b, head_w, head_b = pl.pallas_call(
        kernel,
        out_shape=(
            jax.ShapeDtypeStruct(features.shape, BF16),
            jax.ShapeDtypeStruct((9, 64, 64), F32),
            jax.ShapeDtypeStruct((1, 64), F32),
            jax.ShapeDtypeStruct((NB, 64), F32),
            jax.ShapeDtypeStruct((1, NB), F32),
        ),
        in_specs=[vmem] * 8,
        out_specs=(vmem,) * 5,
        scratch_shapes=scratch,
        compiler_params=pltpu.CompilerParams(collective_id=1, has_side_effects=True),
        name="pair_head",
    )(
        features,
        conv_weight.reshape(9, 64, 64),
        conv_bias.reshape(1, 64),
        head_weight,
        head_bias.reshape(1, NB),
        dist_label,
        omega_label,
        residue_mask.reshape(16, 128),
    )
    return (
        grad_input,
        conv_w.reshape(3, 3, 64, 64),
        conv_b.reshape(64),
        head_w,
        head_b.reshape(NB),
    )


def solution(mesh):
    return jax.shard_map(
        per_device,
        mesh=mesh,
        in_specs=(P(None, "col", "row"), P(), P(), P(), P(), P("col", "row"), P("col", "row"), P()),
        out_specs=(P(None, "col", "row"), P(), P(), P(), P()),
        check_vma=False,
    )
```

```python
import functools

import jax
import jax.numpy as jnp
from jax import lax
from jax.experimental import pallas as pl
from jax.experimental.pallas import tpu as pltpu
from jax.sharding import PartitionSpec as P

MESH = pl.DeviceIdType.MESH
F32 = jnp.float32
BF16 = jnp.bfloat16
DB = 37
NB = 62
RIM_SEMS = (
    "band_send", "band_recv", "edge_send", "edge_recv", "via_send", "via_recv",
    "relay_send", "corner_send", "corner_recv",
)

def device(x, y, z, core):
    return ((z // 4) * 4 + x, (y * 4 + lax.rem(z, 4)) * 2 + core)


class Place:
    def __init__(self):
        self.row = lax.axis_index("row")
        self.col = lax.axis_index("col")
        self.x = lax.rem(self.row, 4)
        self.core = lax.rem(self.col, 2)
        chip = self.col // 2
        self.y = chip // 4
        self.block = self.row // 4
        self.z = 4 * self.block + lax.rem(chip, 4)
        self.spot = 4 * self.y + self.x

    def is_me(self, t):
        return (t[0] == self.x) & (t[1] == self.y) & (t[2] == self.z) & (t[3] == self.core)

    def mirror_first(self, k):
        return (lax.rem(k, 4), k // 4, self.z, self.core)

    def mirror_second(self, s, half):
        return (lax.rem(self.z, 4), self.z // 4, s, half)

    def mirror_giver(self, k, core):
        return (lax.rem(k, 4), k // 4, self.spot, core)

    def plane(self, s):
        return (lax.rem(s // 2, 4), s // 8, self.z, lax.rem(s, 2))

    def plane_slot(self):
        return self.spot * 2 + self.core

    def ring(self, z):
        return (self.x, self.y, z, self.core)


def signal(barrier, target):
    pl.semaphore_signal(barrier, inc=1, device_id=target, device_id_type=MESH)


def next_along_row(me, flow):
    return (me.row + 1, me.col) if flow == 0 else (me.row - 1, me.col)


def near(me, flow):
    return me.x < 3 if flow == 0 else me.x > 0


def far_open(me, flow):
    return me.block < 3 if flow == 0 else me.block > 0


def far_source(flow):
    return 3 if flow == 0 else 0


def far_target(me, flow):
    if flow == 0:
        return device(0, me.y, me.z + 4, me.core)
    return device(3, me.y, me.z - 4, me.core)


def receives(me, flow):
    return me.row > 0 if flow == 0 else me.row < 15


def col_open(me, side):
    return me.col > 0 if side == 0 else me.col < 31


def next_along_col(me, side):
    return (me.row, me.col - 1) if side == 0 else (me.row, me.col + 1)


def greet(me, barrier):
    for side in range(2):
        @pl.when(col_open(me, side))
        def _():
            signal(barrier, next_along_col(me, side))

    for flow in range(2):
        @pl.when(near(me, flow))
        def _():
            signal(barrier, next_along_row(me, flow))

    def far_partners(k, carry):
        @pl.when((me.x == 0) & (me.block > 0))
        def _():
            signal(barrier, device(k, me.y, me.z - 4, me.core))

        @pl.when((me.x == 3) & (me.block < 3))
        def _():
            signal(barrier, device(k, me.y, me.z + 4, me.core))
        return carry

    lax.fori_loop(0, 4, far_partners, 0)

    def mirror_partners(s, carry):
        for t in (me.mirror_first(s), me.mirror_giver(s, 0), me.mirror_giver(s, 1)):
            @pl.when(jnp.logical_not(me.is_me(t)))
            def _():
                signal(barrier, device(*t))
        return carry

    lax.fori_loop(0, 16, mirror_partners, 0)

    def plane_partners(t, carry):
        signal(barrier, device(*me.plane(lax.rem(me.plane_slot() + t, 32))))
        return carry

    lax.fori_loop(1, 32, plane_partners, 0)

    def ring_partners(t, carry):
        signal(barrier, device(*me.ring(lax.rem(me.z + t, 16))))
        return carry

    lax.fori_loop(1, 16, ring_partners, 0)


def await_greetings(me, barrier):
    total = 46 + 47 - jnp.where(me.spot == me.z, 1, 0)
    for k in range(2):
        for known in (col_open(me, k), near(me, k), far_open(me, k)):
            total = total + jnp.where(known, 1, 0)
    pl.semaphore_wait(barrier, total)


def remote(source, target, sent, arrived, to):
    return pltpu.make_async_remote_copy(
        src_ref=source, dst_ref=target, send_sem=sent, recv_sem=arrived,
        device_id=to, device_id_type=MESH,
    )


def edge(refs, flow, k):
    return refs[("right", "left")[flow]].at[pl.ds(2 * k, 2)]


def rim(refs, flow, k):
    return refs[("from_left", "from_right")[flow]].at[pl.ds(2 * k + 2, 2)]


def band_copy(me, refs, sems, side):
    first, into = ((16, 80), (64, 0))[side]
    return remote(
        refs["own"].at[pl.ds(first, 16)], refs["own"].at[pl.ds(into, 16)],
        sems["band_send"].at[side], sems["band_recv"].at[side], next_along_col(me, side),
    )


def edge_copy(me, refs, sems, flow, k, to):
    return remote(
        edge(refs, flow, k), rim(refs, flow, k),
        sems["edge_send"].at[flow, k], sems["edge_recv"].at[flow, k], to,
    )


def via_copy(me, refs, sems, flow, k):
    return remote(
        edge(refs, flow, k), refs["via"].at[flow],
        sems["via_send"].at[flow, k], sems["via_recv"].at[flow],
        device(k, me.y, me.z, me.core),
    )


def relay_copy(me, refs, sems, flow):
    return remote(
        refs["via"].at[flow], rim(refs, flow, me.x),
        sems["relay_send"].at[flow], sems["edge_recv"].at[flow, me.x], far_target(me, flow),
    )


def corner_copy(me, refs, sems, flow, side):
    held = refs[("from_left", "from_right")[flow]]
    first, into = ((2, 10), (8, 0))[side]
    return remote(
        held.at[pl.ds(first, 2)], held.at[pl.ds(into, 2)],
        sems["corner_send"].at[flow, side], sems["corner_recv"].at[flow, side],
        next_along_col(me, side),
    )


def send_rims(me, refs, sems):
    for flow in range(2):
        own = far_source(flow)

        @pl.when((me.x == own) & far_open(me, flow))
        def _():
            for k in range(4):
                if k != own:
                    via_copy(me, refs, sems, flow, k).start()
            edge_copy(me, refs, sems, flow, own, far_target(me, flow)).start()

        @pl.when(near(me, flow))
        def _():
            for k in range(4):
                edge_copy(me, refs, sems, flow, k, next_along_row(me, flow)).start()

    for side in range(2):
        @pl.when(col_open(me, side))
        def _():
            band_copy(me, refs, sems, side).start()

        @pl.when(jnp.logical_not(col_open(me, side)))
        def _():
            into = (0, 80)[side]
            refs["own"][into : into + 16] = jnp.zeros((16, 64, 128), BF16)
            into = (0, 10)[side]
            refs["from_left"][into : into + 2] = jnp.zeros((2, 64, 128), BF16)
            refs["from_right"][into : into + 2] = jnp.zeros((2, 64, 128), BF16)

    for flow in range(2):
        @pl.when(jnp.logical_not(receives(me, flow)))
        def _():
            refs[("from_left", "from_right")[flow]][...] = jnp.zeros((12, 64, 128), BF16)


def relay_rims(me, refs, sems):
    for flow in range(2):
        @pl.when((me.x != far_source(flow)) & far_open(me, flow))
        def _():
            via_copy(me, refs, sems, flow, 0).wait_recv()
            relay_copy(me, refs, sems, flow).start()


def await_rims(me, refs, sems):
    for flow in range(2):
        for k in (0, 3, 1, 2):
            @pl.when(receives(me, flow))
            def _():
                edge_copy(me, refs, sems, flow, k, next_along_row(me, flow)).wait_recv()

            if k in (0, 3):
                side = k // 3

                @pl.when(receives(me, flow) & col_open(me, side))
                def _():
                    corner_copy(me, refs, sems, flow, side).start()

    for side in range(2):
        @pl.when(col_open(me, 1 - side))
        def _():
            band_copy(me, refs, sems, side).wait_recv()

        for flow in range(2):
            @pl.when(receives(me, flow) & col_open(me, 1 - side))
            def _():
                corner_copy(me, refs, sems, flow, side).wait_recv()


def await_sent_rims(me, refs, sems):
    for flow in range(2):
        own = far_source(flow)

        @pl.when((me.x == own) & far_open(me, flow))
        def _():
            for k in range(4):
                if k != own:
                    via_copy(me, refs, sems, flow, k).wait_send()
            edge_copy(me, refs, sems, flow, own, far_target(me, flow)).wait_send()

        @pl.when((me.x != own) & far_open(me, flow))
        def _():
            relay_copy(me, refs, sems, flow).wait_send()

        @pl.when(near(me, flow))
        def _():
            for k in range(4):
                edge_copy(me, refs, sems, flow, k, next_along_row(me, flow)).wait_send()

        for side in range(2):
            @pl.when(receives(me, flow) & col_open(me, side))
            def _():
                corner_copy(me, refs, sems, flow, side).wait_send()

    for side in range(2):
        @pl.when(col_open(me, side))
        def _():
            band_copy(me, refs, sems, side).wait_send()


def lanes():
    return lax.broadcasted_iota(jnp.int32, (64, 128), 1)


def turn(v, by):
    by = by % 128
    return v if by == 0 else pltpu.roll(v, by, 1)


def gather_edges(rows, left, right, at):
    group = lanes() // 16
    low = turn(rows[0], 0)
    high = turn(rows[0], 16)
    for g in range(1, 8):
        low = jnp.where(group == g, turn(rows[g], 16 * g), low)
        high = jnp.where(group == g, turn(rows[g], 16 * (g + 1)), high)
    left[at] = low.astype(BF16)
    right[at] = high.astype(BF16)


def stack_taps(refs, stack, first, last):
    lane = lanes()

    def eight(at, carry):
        before = refs["from_left"][at].astype(F32)
        after = refs["from_right"][at].astype(F32)
        for g in range(8):
            e = at * 8 + g
            cells = refs["own"][e]
            c32 = cells.astype(F32)
            lower = jnp.where(lane < 16, turn(before, -16 * g), turn(c32, 16))
            upper = jnp.where(lane >= 112, turn(after, 112 - 16 * g), turn(c32, 112))
            stack[e, 0:64] = lower.astype(BF16)
            stack[e, 64:128] = cells
            stack[e, 128:192] = upper.astype(BF16)
        return carry

    lax.fori_loop(first, last, eight, 0)


def window(stack, at):
    return jnp.concatenate(
        [
            jnp.concatenate([stack[at * 8 + r + 16 * a] for a in range(3)], axis=0)
            for r in range(8)
        ],
        axis=1,
    )


def rows_of(ref, at):
    return jnp.concatenate([ref[at * 8 + r] for r in range(8)], axis=1)


def strided(i):
    return pl.ds(i, 64, stride=64)


def block(n, at):
    return pl.ds(pl.multiple_of(n * 64 + at * 8, 8), 8)


def kernel(
    feat, cw, cb, wh, hb, dist, omega, mask,
    grad_out, sums_out,
    flat, logit, held, own, left, right, from_left, from_right, via, stack, mixed,
    gown, gleft, gright, gfrom_left, gfrom_right, gvia, grads, glogit,
    wc, wf, whp, wht, bias_c, bias_h,
    packed, tmp, placed, sums, rows, src, parts, mine, whole, ring, dst,
    a_send, a_recv, b_send, b_recv,
    send_1, recv_1, send_2, recv_2, send_3, recv_3,
    *rim_sems,
):
    act_sems = dict(zip(RIM_SEMS, rim_sems[:9]))
    grad_sems = dict(zip(RIM_SEMS, rim_sems[9:]))
    me = Place()
    barrier = pltpu.get_barrier_semaphore()
    greet(me, barrier)
    act = dict(own=own, left=left, right=right, from_left=from_left, from_right=from_right, via=via)
    grd = dict(own=gown, left=gleft, right=gright, from_left=gfrom_left, from_right=gfrom_right, via=gvia)

    def widen(c, carry):
        flat[pl.ds(pl.multiple_of(c * 64, 64), 64), :] = feat[c].astype(F32)
        return carry

    lax.fori_loop(0, 64, widen, 0)

    def activate(at, carry):
        rounded = []
        for g in range(8):
            i = at * 8 + g
            v = flat[strided(i), :]
            held[i] = v.astype(BF16)
            cells = jnp.where(v > 0.0, v, jnp.exp(jnp.minimum(v, 0.0)) - 1.0).astype(BF16)
            own[16 + i] = cells
            rounded.append(cells.astype(F32))
        gather_edges(rounded, left, right, at)
        return carry

    lax.fori_loop(0, 8, activate, 0)
    await_greetings(me, barrier)
    send_rims(me, act, act_sems)

    relay_rims(me, act, act_sems)

    for k in range(9):
        wc[:, 64 * k : 64 * k + 64] = cw[k]
        wf[:, 64 * k : 64 * k + 64] = cw[8 - k].astype(F32).T.astype(BF16)
    whp[...] = jnp.zeros((64, 64), BF16)
    whp[0:NB, :] = wh[...]
    wht[...] = whp[...].astype(F32).T.astype(BF16)
    bias_c[...] = jnp.broadcast_to(cb[...], (128, 64)).T
    bias_h[...] = jnp.zeros((64, 128), F32)
    bias_h[0:NB, :] = jnp.broadcast_to(hb[...], (128, NB)).T

    await_rims(me, act, act_sems)

    def forward(at, carry):
        pre = jnp.dot(wc[...], window(stack, at), preferred_element_type=F32)
        pre = pre + jnp.concatenate([bias_c[...]] * 8, axis=1)
        mix = (rows_of(held, at).astype(F32) + pre).astype(BF16)
        out = jnp.dot(whp[...], mix, preferred_element_type=F32)
        out = (out + jnp.concatenate([bias_h[...]] * 8, axis=1)).astype(BF16).astype(F32)
        for r in range(8):
            mixed[at * 8 + r] = mix[:, 128 * r : 128 * r + 128]
            logit[strided(at * 8 + r), :] = out[:, 128 * r : 128 * r + 128]
        return carry

    def pack(part):
        low = lax.broadcasted_iota(jnp.int32, (32, 128), 1) < 64
        at = 32 * part

        def step(m, carry):
            one = logit[pl.ds(pl.multiple_of(m * 64 + at, 32), 32), :]
            two = logit[pl.ds(pl.multiple_of(m * 64 + 2048 + at, 32), 32), :]
            packed[0, m, at : at + 32] = jnp.where(low, one, turn(two, 64)).astype(BF16)
            packed[1, m, at : at + 32] = jnp.where(low, turn(one, 64), two).astype(BF16)
            return carry

        lax.fori_loop(0, 32, step, 0)

    def piece(ref, h, k, part):
        return ref.at[h, pl.ds(k * 2, 2), pl.ds(32 * part, 32)]

    apart = lax.rem(me.spot - me.z + 16, 16)
    apart = lax.rem(jnp.minimum(apart, 16 - apart), 8)

    def mirror_a(part):
        def step(t, carry):
            k = lax.rem(apart - t // 2 + 8, 8) + 8 * lax.rem(t, 2)
            to = me.mirror_first(k)
            for h in range(2):
                @pl.when(me.is_me(to))
                def _():
                    pltpu.make_async_copy(
                        piece(packed, h, k, part), tmp.at[part, me.spot, h],
                        a_recv.at[part, me.spot, h],
                    ).start()

                @pl.when(jnp.logical_not(me.is_me(to)))
                def _():
                    remote(
                        piece(packed, h, k, part), tmp.at[part, me.spot, h],
                        a_send.at[part, k, h], a_recv.at[part, me.spot, h], device(*to),
                    ).start()
            return carry

        lax.fori_loop(0, 16, step, 0)

    def mirror_b(part, t):
        p = lax.rem(me.spot + t // 2, 8)
        back = jnp.where(p == 0, 8, 16 - p)
        s = lax.rem(me.z + jnp.where(lax.rem(t, 2) == 0, p, back), 16)
        for h in range(2):
            pltpu.make_async_copy(
                piece(packed, h, 0, part), tmp.at[part, s, h], a_recv.at[part, s, h]
            ).wait()
            to = me.mirror_second(s, h)

            @pl.when(me.is_me(to))
            def _():
                pltpu.make_async_copy(
                    tmp.at[part, s, h], piece(placed, me.core, me.spot, part),
                    b_recv.at[part, me.core, me.spot],
                ).start()

            @pl.when(jnp.logical_not(me.is_me(to)))
            def _():
                remote(
                    tmp.at[part, s, h], piece(placed, me.core, me.spot, part),
                    b_send.at[part, s, h], b_recv.at[part, me.core, me.spot], device(*to),
                ).start()

    stack_taps(act, stack, 0, 8)
    lax.fori_loop(0, 4, forward, 0)
    pack(0)
    mirror_a(0)
    stack_taps(act, stack, 8, 12)

    def forward_and_pass(at, carry):
        forward(at, carry)

        def pass_on(u, inner):
            mirror_b(0, (at - 4) * 4 + u)
            return inner

        lax.fori_loop(0, 4, pass_on, 0)
        return carry

    lax.fori_loop(4, 8, forward_and_pass, 0)
    pack(1)
    mirror_a(1)

    def pass_rest(t, carry):
        mirror_b(1, t)
        return carry

    lax.fori_loop(0, 16, pass_rest, 0)

    mine_first = mask[pl.ds(me.col // 2, 1), :].astype(F32)
    mine_first = jnp.broadcast_to(mine_first, (128, 128)).T
    first = jnp.where(me.core == 0, mine_first[0:64], mine_first[64:128])
    pair = first * mask[pl.ds(me.row, 1), :].astype(F32)

    def arrive(k, carry):
        for c in range(2):
            for part in range(2):
                pltpu.make_async_copy(
                    tmp.at[part, 0, 0], piece(placed, c, k, part), b_recv.at[part, c, k]
                ).wait()
        for u in range(2):
            m = k * 2 + u
            other = jnp.concatenate([placed[0, m], placed[1, m]], axis=0).astype(F32).T
            one = pl.ds(pl.multiple_of(m * 64, 64), 64)
            two = pl.ds(pl.multiple_of(m * 64 + 2048, 64), 64)
            flat[one, :] = 0.5 * (logit[one, :] + other[0:64])
            flat[two, :] = 0.5 * (logit[two, :] + other[64:128])
        return carry

    lax.fori_loop(0, 16, arrive, 0)
    sums[0] = pair

    def softmaxes(at, carry):
        eight = pl.ds(pl.multiple_of(at * 8, 8), 8)
        weight = sums[0, eight, :]
        for start, stop, label in ((0, DB, dist), (DB, NB, omega)):
            chosen = label[eight, :]
            top = flat[block(start, at), :]
            for n in range(start + 1, stop):
                top = jnp.maximum(top, flat[block(n, at), :])
            below = jnp.zeros((8, 128), F32)
            for n in range(start, stop):
                e = jnp.exp(flat[block(n, at), :] - top)
                flat[block(n, at), :] = e
                below = below + e
            scale = 1.0 / below
            for n in range(start, stop):
                hot = jnp.where(chosen == n - start, 1.0, 0.0)
                flat[block(n, at), :] = weight * (flat[block(n, at), :] * scale - hot)
        for n in range(NB, 64):
            flat[block(n, at), :] = jnp.zeros((8, 128), F32)
        return carry

    lax.fori_loop(0, 8, softmaxes, 0)

    rows[...] = jnp.zeros((64, 640), F32)
    sums[...] = jnp.zeros((2, 64, 128), F32)

    def backward(at, carry):
        per_row = [flat[strided(at * 8 + r), :] for r in range(8)]
        bins = per_row[0]
        for r in range(1, 8):
            bins = bins + per_row[r]
        sums[0] += bins
        for r in range(8):
            glogit[at * 8 + r] = per_row[r].astype(BF16)
        grad_logit = jnp.concatenate([v.astype(BF16) for v in per_row], axis=1)
        back = jnp.dot(wht[...], grad_logit, preferred_element_type=F32)
        pieces = [back[:, 128 * r : 128 * r + 128] for r in range(8)]
        total = pieces[0]
        for r in range(1, 8):
            total = total + pieces[r]
        sums[1] += total
        rounded = []
        for r in range(8):
            grads[at * 8 + r] = pieces[r]
            cells = pieces[r].astype(BF16)
            gown[16 + at * 8 + r] = cells
            rounded.append(cells.astype(F32))
        gather_edges(rounded, gleft, gright, at)
        return carry

    lax.fori_loop(0, 8, backward, 0)
    send_rims(me, grd, grad_sems)

    def weights(at, carry):
        over_pairs = (((1,), (1,)), ((), ()))
        rows[:, 0:576] += lax.dot_general(
            jnp.concatenate([gown[16 + at * 8 + r] for r in range(8)], axis=1),
            window(stack, at), over_pairs, preferred_element_type=F32,
        )
        rows[:, 576:640] += lax.dot_general(
            rows_of(glogit, at), rows_of(mixed, at), over_pairs, preferred_element_type=F32
        )
        return carry

    lax.fori_loop(0, 8, weights, 0)
    relay_rims(me, grd, grad_sems)

    rows[62:63, 576:640] = jnp.sum(sums[1].T, axis=0, keepdims=True)
    rows[63:64, 576:640] = jnp.sum(sums[0].T, axis=0, keepdims=True)
    for t in range(5):
        whole[64 * t : 64 * t + 64, :] = rows[:, 128 * t : 128 * t + 128]
    for s in range(32):
        src[s] = whole[10 * s : 10 * s + 10, :]
    slot = me.plane_slot()

    def send_parts(t, carry):
        s = lax.rem(slot + t, 32)
        pltpu.make_async_remote_copy(
            src_ref=src.at[s], dst_ref=parts.at[slot], send_sem=send_1.at[s],
            recv_sem=recv_1.at[slot], device_id=device(*me.plane(s)), device_id_type=MESH,
        ).start()
        return carry

    lax.fori_loop(1, 32, send_parts, 0)
    parts[slot] = src[slot]

    def wait_parts(t, carry):
        s = lax.rem(slot + t, 32)
        pltpu.make_async_copy(src.at[0], parts.at[s], recv_1.at[s]).wait()
        return carry

    lax.fori_loop(1, 32, wait_parts, 0)
    mine[0] = jnp.sum(parts[...], axis=0)
    ring[me.z] = mine[0]

    def send_ring(t, carry):
        o = lax.rem(me.z + t, 16)
        pltpu.make_async_remote_copy(
            src_ref=mine.at[0], dst_ref=ring.at[me.z], send_sem=send_2.at[o],
            recv_sem=recv_2.at[me.z], device_id=device(*me.ring(o)), device_id_type=MESH,
        ).start()
        return carry

    lax.fori_loop(1, 16, send_ring, 0)

    await_rims(me, grd, grad_sems)
    stack_taps(grd, stack, 0, 12)

    def inputs(at, carry):
        back = jnp.dot(wf[...], window(stack, at), preferred_element_type=F32)
        for r in range(8):
            i = at * 8 + r
            v = held[i].astype(F32)
            slope = jnp.where(v > 0.0, 1.0, jnp.exp(jnp.minimum(v, 0.0)))
            flat[strided(i), :] = grads[i] + slope * back[:, 128 * r : 128 * r + 128]
        return carry

    lax.fori_loop(0, 4, inputs, 0)

    def wait_ring(t, carry):
        o = lax.rem(me.z + t, 16)
        pltpu.make_async_copy(mine.at[0], ring.at[o], recv_2.at[o]).wait()
        return carry

    lax.fori_loop(1, 16, wait_ring, 0)
    mine[1] = jnp.sum(ring[...], axis=0)
    dst[slot] = mine[1]

    def send_all(t, carry):
        s = lax.rem(slot + t, 32)
        pltpu.make_async_remote_copy(
            src_ref=mine.at[1], dst_ref=dst.at[slot], send_sem=send_3.at[s],
            recv_sem=recv_3.at[slot], device_id=device(*me.plane(s)), device_id_type=MESH,
        ).start()
        return carry

    lax.fori_loop(1, 32, send_all, 0)

    lax.fori_loop(4, 8, inputs, 0)

    def narrow(c, carry):
        grad_out[c] = flat[pl.ds(pl.multiple_of(c * 64, 64), 64), :].astype(BF16)
        return carry

    lax.fori_loop(0, 64, narrow, 0)

    def wait_all(t, carry):
        s = lax.rem(slot + t, 32)
        pltpu.make_async_copy(mine.at[1], dst.at[s], recv_3.at[s]).wait()
        return carry

    lax.fori_loop(1, 32, wait_all, 0)
    for s in range(32):
        sums_out[10 * s : 10 * s + 10, :] = dst[s]
    await_sent_rims(me, act, act_sems)
    await_sent_rims(me, grd, grad_sems)

    def sent_mirror(k, carry):
        for h in range(2):
            for part in range(2):
                @pl.when(jnp.logical_not(me.is_me(me.mirror_first(k))))
                def _():
                    pltpu.make_async_copy(
                        piece(packed, h, k, part), tmp.at[part, 0, h], a_send.at[part, k, h]
                    ).wait()

                @pl.when(jnp.logical_not(me.is_me(me.mirror_second(k, h))))
                def _():
                    pltpu.make_async_copy(
                        tmp.at[part, k, h], piece(placed, 0, 0, part), b_send.at[part, k, h]
                    ).wait()
        return carry

    lax.fori_loop(0, 16, sent_mirror, 0)

    def sent_plane(t, carry):
        s = lax.rem(slot + t, 32)
        pltpu.make_async_copy(mine.at[0], dst.at[s], send_1.at[s]).wait()
        pltpu.make_async_copy(mine.at[0], dst.at[s], send_3.at[s]).wait()
        return carry

    lax.fori_loop(1, 32, sent_plane, 0)

    def sent_ring(t, carry):
        o = lax.rem(me.z + t, 16)
        pltpu.make_async_copy(mine.at[0], ring.at[o], send_2.at[o]).wait()
        return carry

    lax.fori_loop(1, 16, sent_ring, 0)


def finish(grad, sums, mask, grad_out, cw_out, cb_out, wh_out, hb_out):
    count = jnp.sum(mask[...].astype(F32), keepdims=True)
    for k in range(9):
        t, half = k // 2, k % 2
        cw_out[k] = sums[64 * t : 64 * t + 64, 64 * half : 64 * half + 64] / count
    wh_out[...] = sums[256 : 256 + NB, 64:128] / count
    cb_out[...] = sums[318:319, 64:128] / count
    hb_out[...] = sums[319:320, 64 : 64 + NB] / count
    grad_out[...] = grad[...]


def per_device(
    features, conv_weight, conv_bias, head_weight, head_bias, dist_label, omega_label, residue_mask
):
    vmem = pl.BlockSpec(memory_space=pltpu.VMEM)
    cells = (64, 128)
    dma = pltpu.SemaphoreType.DMA
    scratch = [
        pltpu.VMEM((4096, 128), F32),
        pltpu.VMEM((4096, 128), F32),
        pltpu.VMEM((64,) + cells, BF16),
        pltpu.VMEM((96,) + cells, BF16),
        pltpu.VMEM((8,) + cells, BF16),
        pltpu.VMEM((8,) + cells, BF16),
        pltpu.VMEM((12,) + cells, BF16),
        pltpu.VMEM((12,) + cells, BF16),
        pltpu.VMEM((2, 2) + cells, BF16),
        pltpu.VMEM((96, 192, 128), BF16),
        pltpu.VMEM((64,) + cells, BF16),
        pltpu.VMEM((96,) + cells, BF16),
        pltpu.VMEM((8,) + cells, BF16),
        pltpu.VMEM((8,) + cells, BF16),
        pltpu.VMEM((12,) + cells, BF16),
        pltpu.VMEM((12,) + cells, BF16),
        pltpu.VMEM((2, 2) + cells, BF16),
        pltpu.VMEM((64,) + cells, F32),
        pltpu.VMEM((64,) + cells, BF16),
        pltpu.VMEM((64, 576), BF16),
        pltpu.VMEM((64, 576), BF16),
        pltpu.VMEM((64, 64), BF16),
        pltpu.VMEM((64, 64), BF16),
        pltpu.VMEM(cells, F32),
        pltpu.VMEM(cells, F32),
        pltpu.VMEM((2, 32) + cells, BF16),
        pltpu.VMEM((2, 16, 2, 2, 32, 128), BF16),
        pltpu.VMEM((2, 32) + cells, BF16),
        pltpu.VMEM((2,) + cells, F32),
        pltpu.VMEM((64, 640), F32),
        pltpu.VMEM((32, 10, 128), F32),
        pltpu.VMEM((32, 10, 128), F32),
        pltpu.VMEM((2, 10, 128), F32),
        pltpu.VMEM((320, 128), F32),
        pltpu.VMEM((16, 10, 128), F32),
        pltpu.VMEM((32, 10, 128), F32),
        dma((2, 16, 2)), dma((2, 16, 2)), dma((2, 16, 2)), dma((2, 2, 16)),
        dma((32,)), dma((32,)), dma((16,)), dma((16,)), dma((32,)), dma((32,)),
    ] + 2 * [
        dma((2,)), dma((2,)), dma((2, 4)), dma((2, 4)), dma((2, 4)), dma((2,)),
        dma((2,)), dma((2, 2)), dma((2, 2)),
    ]
    present = residue_mask.reshape(16, 128)
    grad, sums = pl.pallas_call(
        kernel,
        out_shape=(
            jax.ShapeDtypeStruct(features.shape, BF16),
            jax.ShapeDtypeStruct((320, 128), F32),
        ),
        in_specs=[vmem] * 8,
        out_specs=(vmem,) * 2,
        scratch_shapes=scratch,
        compiler_params=pltpu.CompilerParams(collective_id=1, has_side_effects=True),
        name="pair_head",
    )(
        features,
        conv_weight.reshape(9, 64, 64),
        conv_bias.reshape(1, 64),
        head_weight,
        head_bias.reshape(1, NB),
        dist_label,
        omega_label,
        present,
    )
    grad_input, conv_w, conv_b, head_w, head_b = pl.pallas_call(
        finish,
        out_shape=(
            jax.ShapeDtypeStruct(features.shape, BF16),
            jax.ShapeDtypeStruct((9, 64, 64), F32),
            jax.ShapeDtypeStruct((1, 64), F32),
            jax.ShapeDtypeStruct((NB, 64), F32),
            jax.ShapeDtypeStruct((1, NB), F32),
        ),
        in_specs=[vmem] * 3,
        out_specs=(vmem,) * 5,
        name="scale",
    )(grad, sums, present)
    return (
        grad_input,
        conv_w.reshape(3, 3, 64, 64),
        conv_b.reshape(64),
        head_w,
        head_b.reshape(NB),
    )


def solution(mesh):
    return jax.shard_map(
        per_device,
        mesh=mesh,
        in_specs=(P(None, "col", "row"), P(), P(), P(), P(), P("col", "row"), P("col", "row"), P()),
        out_specs=(P(None, "col", "row"), P(), P(), P(), P()),
        check_vma=False,
    )
```

```python
import functools

import jax
import jax.numpy as jnp
from jax import lax
from jax.experimental import pallas as pl
from jax.experimental.pallas import tpu as pltpu
from jax.sharding import PartitionSpec as P

MESH = pl.DeviceIdType.MESH
F32 = jnp.float32
BF16 = jnp.bfloat16
DB = 37
NB = 62
RIM_SEMS = (
    "band_send", "band_recv", "edge_send", "edge_recv", "via_send", "via_recv",
    "relay_send", "corner_send", "corner_recv",
)

def device(x, y, z, core):
    return ((z // 4) * 4 + x, (y * 4 + lax.rem(z, 4)) * 2 + core)


class Place:
    def __init__(self):
        self.row = lax.axis_index("row")
        self.col = lax.axis_index("col")
        self.x = lax.rem(self.row, 4)
        self.core = lax.rem(self.col, 2)
        chip = self.col // 2
        self.y = chip // 4
        self.block = self.row // 4
        self.z = 4 * self.block + lax.rem(chip, 4)
        self.spot = 4 * self.y + self.x

    def mirrors_itself(self):
        return self.spot == self.z

    def mirror_first(self, k):
        return (lax.rem(k, 4), k // 4, self.z, self.core)

    def mirror_second(self, s, half):
        return (lax.rem(self.z, 4), self.z // 4, s, half)

    def plane(self, s):
        return (lax.rem(s // 2, 4), s // 8, self.z, lax.rem(s, 2))

    def plane_slot(self):
        return self.spot * 2 + self.core

    def ring(self, z):
        return (self.x, self.y, z, self.core)


def signal(barrier, target):
    pl.semaphore_signal(barrier, inc=1, device_id=target, device_id_type=MESH)


def next_along_row(me, flow):
    return (me.row + 1, me.col) if flow == 0 else (me.row - 1, me.col)


def near(me, flow):
    return me.x < 3 if flow == 0 else me.x > 0


def far_open(me, flow):
    return me.block < 3 if flow == 0 else me.block > 0


def far_source(flow):
    return 3 if flow == 0 else 0


def far_target(me, flow):
    if flow == 0:
        return device(0, me.y, me.z + 4, me.core)
    return device(3, me.y, me.z - 4, me.core)


def receives(me, flow):
    return me.row > 0 if flow == 0 else me.row < 15


def col_open(me, side):
    return me.col > 0 if side == 0 else me.col < 31


def next_along_col(me, side):
    return (me.row, me.col - 1) if side == 0 else (me.row, me.col + 1)


def greet(me, barrier):
    for side in range(2):
        @pl.when(col_open(me, side))
        def _():
            signal(barrier, next_along_col(me, side))

    for flow in range(2):
        @pl.when(near(me, flow))
        def _():
            signal(barrier, next_along_row(me, flow))

    def far_partners(k, carry):
        @pl.when((me.x == 0) & (me.block > 0))
        def _():
            signal(barrier, device(k, me.y, me.z - 4, me.core))

        @pl.when((me.x == 3) & (me.block < 3))
        def _():
            signal(barrier, device(k, me.y, me.z + 4, me.core))
        return carry

    lax.fori_loop(0, 4, far_partners, 0)

    spot_row, spot_col = (me.z // 4) * 4, 2 * lax.rem(me.z, 4)
    giver_row, giver_col = 4 * me.y, 2 * me.x
    for k in range(16):
        for core in range(2):
            @pl.when(jnp.logical_not((me.spot == k) & (me.core == core)))
            def _():
                signal(barrier, (spot_row + k % 4, spot_col + 8 * (k // 4) + core))

            @pl.when(jnp.logical_not(me.mirrors_itself() & (me.spot == k) & (me.core == core)))
            def _():
                signal(barrier, (giver_row + k % 4, giver_col + 8 * (k // 4) + core))

        @pl.when(me.z != k)
        def _():
            signal(barrier, (me.x + 4 * (k // 4), 8 * me.y + 2 * (k % 4) + me.core))


def await_greetings(me, barrier):
    total = 31 + 15 + 32 - jnp.where(me.mirrors_itself(), 1, 0)
    for k in range(2):
        for known in (col_open(me, k), near(me, k), far_open(me, k)):
            total = total + jnp.where(known, 1, 0)
    pl.semaphore_wait(barrier, total)


def remote(source, target, sent, arrived, to):
    return pltpu.make_async_remote_copy(
        src_ref=source, dst_ref=target, send_sem=sent, recv_sem=arrived,
        device_id=to, device_id_type=MESH,
    )


def edge(refs, flow, k):
    return refs[("right", "left")[flow]].at[pl.ds(2 * k, 2)]


def rim(refs, flow, k):
    return refs[("from_left", "from_right")[flow]].at[pl.ds(2 * k + 2, 2)]


def band_copy(me, refs, sems, side):
    first, into = ((16, 80), (64, 0))[side]
    return remote(
        refs["own"].at[pl.ds(first, 16)], refs["own"].at[pl.ds(into, 16)],
        sems["band_send"].at[side], sems["band_recv"].at[side], next_along_col(me, side),
    )


def edge_copy(me, refs, sems, flow, k, to):
    return remote(
        edge(refs, flow, k), rim(refs, flow, k),
        sems["edge_send"].at[flow, k], sems["edge_recv"].at[flow, k], to,
    )


def via_copy(me, refs, sems, flow, k):
    return remote(
        edge(refs, flow, k), refs["via"].at[flow],
        sems["via_send"].at[flow, k], sems["via_recv"].at[flow],
        device(k, me.y, me.z, me.core),
    )


def relay_copy(me, refs, sems, flow):
    return remote(
        refs["via"].at[flow], rim(refs, flow, me.x),
        sems["relay_send"].at[flow], sems["edge_recv"].at[flow, me.x], far_target(me, flow),
    )


def corner_copy(me, refs, sems, flow, side):
    held = refs[("from_left", "from_right")[flow]]
    first, into = ((2, 10), (8, 0))[side]
    return remote(
        held.at[pl.ds(first, 2)], held.at[pl.ds(into, 2)],
        sems["corner_send"].at[flow, side], sems["corner_recv"].at[flow, side],
        next_along_col(me, side),
    )


def send_rims(me, refs, sems):
    for flow in range(2):
        own = far_source(flow)

        @pl.when((me.x == own) & far_open(me, flow))
        def _():
            for k in range(4):
                if k != own:
                    via_copy(me, refs, sems, flow, k).start()
            edge_copy(me, refs, sems, flow, own, far_target(me, flow)).start()

        @pl.when(near(me, flow))
        def _():
            for k in range(4):
                edge_copy(me, refs, sems, flow, k, next_along_row(me, flow)).start()

    for side in range(2):
        @pl.when(col_open(me, side))
        def _():
            band_copy(me, refs, sems, side).start()

        @pl.when(jnp.logical_not(col_open(me, side)))
        def _():
            into = (0, 80)[side]
            refs["own"][into : into + 16] = jnp.zeros((16, 64, 128), BF16)
            into = (0, 10)[side]
            refs["from_left"][into : into + 2] = jnp.zeros((2, 64, 128), BF16)
            refs["from_right"][into : into + 2] = jnp.zeros((2, 64, 128), BF16)

    for flow in range(2):
        @pl.when(jnp.logical_not(receives(me, flow)))
        def _():
            refs[("from_left", "from_right")[flow]][...] = jnp.zeros((12, 64, 128), BF16)


def relay_rims(me, refs, sems):
    for flow in range(2):
        @pl.when((me.x != far_source(flow)) & far_open(me, flow))
        def _():
            via_copy(me, refs, sems, flow, 0).wait_recv()
            relay_copy(me, refs, sems, flow).start()


def await_rims(me, refs, sems):
    for flow in range(2):
        for k in (0, 3, 1, 2):
            @pl.when(receives(me, flow))
            def _():
                edge_copy(me, refs, sems, flow, k, next_along_row(me, flow)).wait_recv()

            if k in (0, 3):
                side = k // 3

                @pl.when(receives(me, flow) & col_open(me, side))
                def _():
                    corner_copy(me, refs, sems, flow, side).start()

    for side in range(2):
        @pl.when(col_open(me, 1 - side))
        def _():
            band_copy(me, refs, sems, side).wait_recv()

        for flow in range(2):
            @pl.when(receives(me, flow) & col_open(me, 1 - side))
            def _():
                corner_copy(me, refs, sems, flow, side).wait_recv()


def await_sent_rims(me, refs, sems):
    for flow in range(2):
        own = far_source(flow)

        @pl.when((me.x == own) & far_open(me, flow))
        def _():
            for k in range(4):
                if k != own:
                    via_copy(me, refs, sems, flow, k).wait_send()
            edge_copy(me, refs, sems, flow, own, far_target(me, flow)).wait_send()

        @pl.when((me.x != own) & far_open(me, flow))
        def _():
            relay_copy(me, refs, sems, flow).wait_send()

        @pl.when(near(me, flow))
        def _():
            for k in range(4):
                edge_copy(me, refs, sems, flow, k, next_along_row(me, flow)).wait_send()

        for side in range(2):
            @pl.when(receives(me, flow) & col_open(me, side))
            def _():
                corner_copy(me, refs, sems, flow, side).wait_send()

    for side in range(2):
        @pl.when(col_open(me, side))
        def _():
            band_copy(me, refs, sems, side).wait_send()


def lanes():
    return lax.broadcasted_iota(jnp.int32, (64, 128), 1)


def turn(v, by):
    by = by % 128
    return v if by == 0 else pltpu.roll(v, by, 1)


def gather_edges(rows, left, right, at):
    group = lanes() // 16
    low = turn(rows[0], 0)
    high = turn(rows[0], 16)
    for g in range(1, 8):
        low = jnp.where(group == g, turn(rows[g], 16 * g), low)
        high = jnp.where(group == g, turn(rows[g], 16 * (g + 1)), high)
    left[at] = low.astype(BF16)
    right[at] = high.astype(BF16)


def stack_taps(refs, stack, first, last):
    lane = lanes()

    def eight(at, carry):
        before = refs["from_left"][at].astype(F32)
        after = refs["from_right"][at].astype(F32)
        for g in range(8):
            e = at * 8 + g
            cells = refs["own"][e]
            c32 = cells.astype(F32)
            lower = jnp.where(lane < 16, turn(before, -16 * g), turn(c32, 16))
            upper = jnp.where(lane >= 112, turn(after, 112 - 16 * g), turn(c32, 112))
            stack[e, 0:64] = lower.astype(BF16)
            stack[e, 64:128] = cells
            stack[e, 128:192] = upper.astype(BF16)
        return carry

    lax.fori_loop(first, last, eight, 0)


def window(stack, at):
    return jnp.concatenate(
        [
            jnp.concatenate([stack[at * 8 + r + 16 * a] for a in range(3)], axis=0)
            for r in range(8)
        ],
        axis=1,
    )


def rows_of(ref, at):
    return jnp.concatenate([ref[at * 8 + r] for r in range(8)], axis=1)


def strided(i):
    return pl.ds(i, 64, stride=64)


def block(n, at):
    return pl.ds(pl.multiple_of(n * 64 + at * 8, 8), 8)


def kernel(
    feat, cw, cb, wh, hb, dist, omega, mask,
    grad_out, sums_out,
    flat, logit, held, own, left, right, from_left, from_right, via, stack, mixed,
    gown, gleft, gright, gfrom_left, gfrom_right, gvia, grads, glogit,
    wc, wf, whp, wht, bias_c, bias_h,
    packed, tmp, placed, sums, rows, src, parts, mine, whole, ring, dst,
    a_send, a_recv, b_send, b_recv,
    send_1, recv_1, send_2, recv_2, send_3, recv_3,
    *rim_sems,
):
    act_sems = dict(zip(RIM_SEMS, rim_sems[:9]))
    grad_sems = dict(zip(RIM_SEMS, rim_sems[9:]))
    me = Place()
    barrier = pltpu.get_barrier_semaphore()
    greet(me, barrier)
    act = dict(own=own, left=left, right=right, from_left=from_left, from_right=from_right, via=via)
    grd = dict(own=gown, left=gleft, right=gright, from_left=gfrom_left, from_right=gfrom_right, via=gvia)

    def widen(c, carry):
        flat[pl.ds(pl.multiple_of(c * 64, 64), 64), :] = feat[c].astype(F32)
        return carry

    lax.fori_loop(0, 64, widen, 0)

    def activate(at, carry):
        rounded = []
        for g in range(8):
            i = at * 8 + g
            v = flat[strided(i), :]
            held[i] = v.astype(BF16)
            cells = jnp.where(v > 0.0, v, jnp.exp(jnp.minimum(v, 0.0)) - 1.0).astype(BF16)
            own[16 + i] = cells
            rounded.append(cells.astype(F32))
        gather_edges(rounded, left, right, at)
        return carry

    lax.fori_loop(0, 8, activate, 0)
    await_greetings(me, barrier)
    send_rims(me, act, act_sems)

    relay_rims(me, act, act_sems)

    for k in range(9):
        wc[:, 64 * k : 64 * k + 64] = cw[k]
        wf[:, 64 * k : 64 * k + 64] = cw[8 - k].astype(F32).T.astype(BF16)
    whp[...] = jnp.zeros((64, 64), BF16)
    whp[0:NB, :] = wh[...]
    wht[...] = whp[...].astype(F32).T.astype(BF16)
    bias_c[...] = jnp.broadcast_to(cb[...], (128, 64)).T
    bias_h[...] = jnp.zeros((64, 128), F32)
    bias_h[0:NB, :] = jnp.broadcast_to(hb[...], (128, NB)).T

    await_rims(me, act, act_sems)

    def forward(at, carry):
        pre = jnp.dot(wc[...], window(stack, at), preferred_element_type=F32)
        pre = pre + jnp.concatenate([bias_c[...]] * 8, axis=1)
        mix = (rows_of(held, at).astype(F32) + pre).astype(BF16)
        out = jnp.dot(whp[...], mix, preferred_element_type=F32)
        out = (out + jnp.concatenate([bias_h[...]] * 8, axis=1)).astype(BF16).astype(F32)
        for r in range(8):
            mixed[at * 8 + r] = mix[:, 128 * r : 128 * r + 128]
            logit[strided(at * 8 + r), :] = out[:, 128 * r : 128 * r + 128]
        return carry

    def pack(half):
        group = lax.broadcasted_iota(jnp.int32, (32, 128), 1) // 32
        at = 32 * half

        def step(m, carry):
            four = [
                logit[pl.ds(pl.multiple_of(m * 64 + 1024 * q + at, 32), 32), :] for q in range(4)
            ]
            for g in range(4):
                out = turn(four[0], -32 * g)
                for q in range(1, 4):
                    out = jnp.where(group == q, turn(four[q], 32 * (q - g)), out)
                packed[g // 2, g % 2, m, at : at + 32] = out.astype(BF16)
            return carry

        lax.fori_loop(0, 16, step, 0)

    def piece(ref, h, k, part):
        return ref.at[h, lax.rem(part, 2), k, pl.ds(pl.multiple_of(32 * (part // 2), 32), 32)]

    apart = lax.rem(me.spot - me.z + 16, 16)
    apart = lax.rem(jnp.minimum(apart, 16 - apart), 8)

    def mirror_a(at, carry):
        part, t = at // 16, lax.rem(at, 16)
        k = lax.rem(apart - t // 2 + 8, 8) + 8 * lax.rem(t, 2)
        to = device(*me.mirror_first(k))
        for h in range(2):
            @pl.when(k == me.spot)
            def _():
                pltpu.make_async_copy(
                    piece(packed, h, k, part), tmp.at[part, me.spot, h],
                    a_recv.at[part, me.spot, h],
                ).start()

            @pl.when(k != me.spot)
            def _():
                remote(
                    piece(packed, h, k, part), tmp.at[part, me.spot, h],
                    a_send.at[part, k, h], a_recv.at[part, me.spot, h], to,
                ).start()
        return carry

    def at_home(s, h):
        return me.mirrors_itself() & (s == me.z) & (me.core == h)

    def mirror_b(at, carry):
        part, t = at // 16, lax.rem(at, 16)
        p = lax.rem(me.spot + t // 2, 8)
        back = jnp.where(p == 0, 8, 16 - p)
        s = lax.rem(me.z + jnp.where(lax.rem(t, 2) == 0, p, back), 16)
        for h in range(2):
            pltpu.make_async_copy(
                piece(packed, h, 0, part), tmp.at[part, s, h], a_recv.at[part, s, h]
            ).wait()

            @pl.when(at_home(s, h))
            def _():
                pltpu.make_async_copy(
                    tmp.at[part, s, h], piece(placed, me.core, me.spot, part),
                    b_recv.at[part, me.core, me.spot],
                ).start()

            @pl.when(jnp.logical_not(at_home(s, h)))
            def _():
                remote(
                    tmp.at[part, s, h], piece(placed, me.core, me.spot, part),
                    b_send.at[part, s, h], b_recv.at[part, me.core, me.spot],
                    device(*me.mirror_second(s, h)),
                ).start()
        return carry

    stack_taps(act, stack, 0, 8)
    lax.fori_loop(0, 4, forward, 0)
    pack(0)
    lax.fori_loop(0, 32, mirror_a, 0)
    stack_taps(act, stack, 8, 12)

    def forward_and_pass(at, carry):
        forward(at, carry)
        return lax.fori_loop((at - 4) * 8, (at - 3) * 8, mirror_b, carry)

    lax.fori_loop(4, 8, forward_and_pass, 0)
    pack(1)
    lax.fori_loop(32, 64, mirror_a, 0)
    lax.fori_loop(32, 64, mirror_b, 0)

    mine_first = mask[pl.ds(me.col // 2, 1), :].astype(F32)
    mine_first = jnp.broadcast_to(mine_first, (128, 128)).T
    first = jnp.where(me.core == 0, mine_first[0:64], mine_first[64:128])
    pair = first * mask[pl.ds(me.row, 1), :].astype(F32)

    sums[...] = jnp.zeros((3, 64, 128), F32)
    sums[2] = pair
    rows[...] = jnp.zeros((64, 640), F32)

    def arrive(half):
        def step(k, carry):
            for c in range(2):
                for here in range(2):
                    part = 2 * here + half
                    pltpu.make_async_copy(
                        tmp.at[part, 0, 0], piece(placed, c, k, part), b_recv.at[part, c, k]
                    ).wait()
            other = jnp.concatenate([placed[0, half, k], placed[1, half, k]], axis=0)
            other = other.astype(F32).T
            for q in range(4):
                at = pl.ds(pl.multiple_of(k * 64 + 1024 * q + 32 * half, 32), 32)
                flat[at, :] = 0.5 * (logit[at, :] + other[32 * q : 32 * q + 32])
            return carry

        lax.fori_loop(0, 16, step, 0)

    def softmaxes(at, carry):
        eight = pl.ds(pl.multiple_of(at * 8, 8), 8)
        weight = sums[2, eight, :]
        for start, stop, label in ((0, DB, dist), (DB, NB, omega)):
            chosen = label[eight, :]
            top = flat[block(start, at), :]
            for n in range(start + 1, stop):
                top = jnp.maximum(top, flat[block(n, at), :])
            below = jnp.zeros((8, 128), F32)
            for n in range(start, stop):
                e = jnp.exp(flat[block(n, at), :] - top)
                flat[block(n, at), :] = e
                below = below + e
            scale = 1.0 / below
            for n in range(start, stop):
                hot = jnp.where(chosen == n - start, 1.0, 0.0)
                flat[block(n, at), :] = weight * (flat[block(n, at), :] * scale - hot)
        for n in range(NB, 64):
            flat[block(n, at), :] = jnp.zeros((8, 128), F32)
        return carry


    def backward(at, carry):
        per_row = [flat[strided(at * 8 + r), :] for r in range(8)]
        bins = per_row[0]
        for r in range(1, 8):
            bins = bins + per_row[r]
        sums[0] += bins
        for r in range(8):
            glogit[at * 8 + r] = per_row[r].astype(BF16)
        grad_logit = jnp.concatenate([v.astype(BF16) for v in per_row], axis=1)
        back = jnp.dot(wht[...], grad_logit, preferred_element_type=F32)
        pieces = [back[:, 128 * r : 128 * r + 128] for r in range(8)]
        total = pieces[0]
        for r in range(1, 8):
            total = total + pieces[r]
        sums[1] += total
        rounded = []
        for r in range(8):
            grads[at * 8 + r] = pieces[r]
            cells = pieces[r].astype(BF16)
            gown[16 + at * 8 + r] = cells
            rounded.append(cells.astype(F32))
        gather_edges(rounded, gleft, gright, at)
        return carry


    def weights(at, carry):
        over_pairs = (((1,), (1,)), ((), ()))
        rows[:, 0:576] += lax.dot_general(
            jnp.concatenate([gown[16 + at * 8 + r] for r in range(8)], axis=1),
            window(stack, at), over_pairs, preferred_element_type=F32,
        )
        rows[:, 576:640] += lax.dot_general(
            rows_of(glogit, at), rows_of(mixed, at), over_pairs, preferred_element_type=F32
        )
        return carry

    arrive(0)
    lax.fori_loop(0, 4, softmaxes, 0)
    lax.fori_loop(0, 4, backward, 0)
    lax.fori_loop(0, 4, weights, 0)
    arrive(1)
    lax.fori_loop(4, 8, softmaxes, 0)
    lax.fori_loop(4, 8, backward, 0)
    send_rims(me, grd, grad_sems)
    lax.fori_loop(4, 8, weights, 0)
    relay_rims(me, grd, grad_sems)

    rows[62:63, 576:640] = jnp.sum(sums[1].T, axis=0, keepdims=True)
    rows[63:64, 576:640] = jnp.sum(sums[0].T, axis=0, keepdims=True)
    for t in range(5):
        whole[64 * t : 64 * t + 64, :] = rows[:, 128 * t : 128 * t + 128]
    for s in range(32):
        src[s] = whole[10 * s : 10 * s + 10, :]
    slot = me.plane_slot()

    def send_parts(t, carry):
        s = lax.rem(slot + t, 32)
        pltpu.make_async_remote_copy(
            src_ref=src.at[s], dst_ref=parts.at[slot], send_sem=send_1.at[s],
            recv_sem=recv_1.at[slot], device_id=device(*me.plane(s)), device_id_type=MESH,
        ).start()
        return carry

    lax.fori_loop(1, 32, send_parts, 0)
    parts[slot] = src[slot]

    await_sent_rims(me, act, act_sems)

    def sent_mirror(at, carry):
        part, k = at // 16, lax.rem(at, 16)
        for h in range(2):
            @pl.when(k != me.spot)
            def _():
                pltpu.make_async_copy(
                    piece(packed, h, k, part), tmp.at[part, 0, h], a_send.at[part, k, h]
                ).wait()

            @pl.when(jnp.logical_not(at_home(k, h)))
            def _():
                pltpu.make_async_copy(
                    tmp.at[part, k, h], piece(placed, 0, 0, part), b_send.at[part, k, h]
                ).wait()
        return carry

    lax.fori_loop(0, 64, sent_mirror, 0)

    def wait_parts(t, carry):
        s = lax.rem(slot + t, 32)
        pltpu.make_async_copy(src.at[0], parts.at[s], recv_1.at[s]).wait()
        return carry

    lax.fori_loop(1, 32, wait_parts, 0)
    mine[0] = jnp.sum(parts[...], axis=0)
    ring[me.z] = mine[0]

    def send_ring(t, carry):
        o = lax.rem(me.z + t, 16)
        pltpu.make_async_remote_copy(
            src_ref=mine.at[0], dst_ref=ring.at[me.z], send_sem=send_2.at[o],
            recv_sem=recv_2.at[me.z], device_id=device(*me.ring(o)), device_id_type=MESH,
        ).start()
        return carry

    lax.fori_loop(1, 16, send_ring, 0)

    await_rims(me, grd, grad_sems)
    stack_taps(grd, stack, 0, 12)

    def inputs(at, carry):
        back = jnp.dot(wf[...], window(stack, at), preferred_element_type=F32)
        for r in range(8):
            i = at * 8 + r
            v = held[i].astype(F32)
            slope = jnp.where(v > 0.0, 1.0, jnp.exp(jnp.minimum(v, 0.0)))
            flat[strided(i), :] = grads[i] + slope * back[:, 128 * r : 128 * r + 128]
        return carry

    lax.fori_loop(0, 4, inputs, 0)

    def wait_ring(t, carry):
        o = lax.rem(me.z + t, 16)
        pltpu.make_async_copy(mine.at[0], ring.at[o], recv_2.at[o]).wait()
        return carry

    lax.fori_loop(1, 16, wait_ring, 0)
    mine[1] = jnp.sum(ring[...], axis=0)
    dst[slot] = mine[1]

    def send_all(t, carry):
        s = lax.rem(slot + t, 32)
        pltpu.make_async_remote_copy(
            src_ref=mine.at[1], dst_ref=dst.at[slot], send_sem=send_3.at[s],
            recv_sem=recv_3.at[slot], device_id=device(*me.plane(s)), device_id_type=MESH,
        ).start()
        return carry

    lax.fori_loop(1, 32, send_all, 0)

    lax.fori_loop(4, 8, inputs, 0)

    def narrow(c, carry):
        grad_out[c] = flat[pl.ds(pl.multiple_of(c * 64, 64), 64), :].astype(BF16)
        return carry

    lax.fori_loop(0, 64, narrow, 0)
    await_sent_rims(me, grd, grad_sems)

    def sent_sums(t, carry):
        s = lax.rem(slot + t, 32)
        pltpu.make_async_copy(mine.at[0], dst.at[s], send_1.at[s]).wait()
        pltpu.make_async_copy(mine.at[0], dst.at[s], send_3.at[s]).wait()
        return carry

    lax.fori_loop(1, 32, sent_sums, 0)

    def sent_ring(t, carry):
        o = lax.rem(me.z + t, 16)
        pltpu.make_async_copy(mine.at[0], ring.at[o], send_2.at[o]).wait()
        return carry

    lax.fori_loop(1, 16, sent_ring, 0)

    def wait_all(t, carry):
        s = lax.rem(slot + t, 32)
        pltpu.make_async_copy(mine.at[1], dst.at[s], recv_3.at[s]).wait()
        return carry

    lax.fori_loop(1, 32, wait_all, 0)
    for s in range(32):
        sums_out[10 * s : 10 * s + 10, :] = dst[s]


def finish(grad, sums, mask, grad_out, cw_out, cb_out, wh_out, hb_out):
    count = jnp.sum(mask[...].astype(F32), keepdims=True)
    for k in range(9):
        t, half = k // 2, k % 2
        cw_out[k] = sums[64 * t : 64 * t + 64, 64 * half : 64 * half + 64] / count
    wh_out[...] = sums[256 : 256 + NB, 64:128] / count
    cb_out[...] = sums[318:319, 64:128] / count
    hb_out[...] = sums[319:320, 64 : 64 + NB] / count
    grad_out[...] = grad[...]


def per_device(
    features, conv_weight, conv_bias, head_weight, head_bias, dist_label, omega_label, residue_mask
):
    vmem = pl.BlockSpec(memory_space=pltpu.VMEM)
    cells = (64, 128)
    dma = pltpu.SemaphoreType.DMA
    scratch = [
        pltpu.VMEM((4096, 128), F32),
        pltpu.VMEM((4096, 128), F32),
        pltpu.VMEM((64,) + cells, BF16),
        pltpu.VMEM((96,) + cells, BF16),
        pltpu.VMEM((8,) + cells, BF16),
        pltpu.VMEM((8,) + cells, BF16),
        pltpu.VMEM((12,) + cells, BF16),
        pltpu.VMEM((12,) + cells, BF16),
        pltpu.VMEM((2, 2) + cells, BF16),
        pltpu.VMEM((96, 192, 128), BF16),
        pltpu.VMEM((64,) + cells, BF16),
        pltpu.VMEM((96,) + cells, BF16),
        pltpu.VMEM((8,) + cells, BF16),
        pltpu.VMEM((8,) + cells, BF16),
        pltpu.VMEM((12,) + cells, BF16),
        pltpu.VMEM((12,) + cells, BF16),
        pltpu.VMEM((2, 2) + cells, BF16),
        pltpu.VMEM((64,) + cells, F32),
        pltpu.VMEM((64,) + cells, BF16),
        pltpu.VMEM((64, 576), BF16),
        pltpu.VMEM((64, 576), BF16),
        pltpu.VMEM((64, 64), BF16),
        pltpu.VMEM((64, 64), BF16),
        pltpu.VMEM(cells, F32),
        pltpu.VMEM(cells, F32),
        pltpu.VMEM((2, 2, 16) + cells, BF16),
        pltpu.VMEM((4, 16, 2, 32, 128), BF16),
        pltpu.VMEM((2, 2, 16) + cells, BF16),
        pltpu.VMEM((3,) + cells, F32),
        pltpu.VMEM((64, 640), F32),
        pltpu.VMEM((32, 10, 128), F32),
        pltpu.VMEM((32, 10, 128), F32),
        pltpu.VMEM((2, 10, 128), F32),
        pltpu.VMEM((320, 128), F32),
        pltpu.VMEM((16, 10, 128), F32),
        pltpu.VMEM((32, 10, 128), F32),
        dma((4, 16, 2)), dma((4, 16, 2)), dma((4, 16, 2)), dma((4, 2, 16)),
        dma((32,)), dma((32,)), dma((16,)), dma((16,)), dma((32,)), dma((32,)),
    ] + 2 * [
        dma((2,)), dma((2,)), dma((2, 4)), dma((2, 4)), dma((2, 4)), dma((2,)),
        dma((2,)), dma((2, 2)), dma((2, 2)),
    ]
    present = residue_mask.reshape(16, 128)
    grad, sums = pl.pallas_call(
        kernel,
        out_shape=(
            jax.ShapeDtypeStruct(features.shape, BF16),
            jax.ShapeDtypeStruct((320, 128), F32),
        ),
        in_specs=[vmem] * 8,
        out_specs=(vmem,) * 2,
        scratch_shapes=scratch,
        compiler_params=pltpu.CompilerParams(collective_id=1, has_side_effects=True),
        name="pair_head",
    )(
        features,
        conv_weight.reshape(9, 64, 64),
        conv_bias.reshape(1, 64),
        head_weight,
        head_bias.reshape(1, NB),
        dist_label,
        omega_label,
        present,
    )
    grad_input, conv_w, conv_b, head_w, head_b = pl.pallas_call(
        finish,
        out_shape=(
            jax.ShapeDtypeStruct(features.shape, BF16),
            jax.ShapeDtypeStruct((9, 64, 64), F32),
            jax.ShapeDtypeStruct((1, 64), F32),
            jax.ShapeDtypeStruct((NB, 64), F32),
            jax.ShapeDtypeStruct((1, NB), F32),
        ),
        in_specs=[vmem] * 3,
        out_specs=(vmem,) * 5,
        name="scale",
    )(grad, sums, present)
    return (
        grad_input,
        conv_w.reshape(3, 3, 64, 64),
        conv_b.reshape(64),
        head_w,
        head_b.reshape(NB),
    )


def solution(mesh):
    return jax.shard_map(
        per_device,
        mesh=mesh,
        in_specs=(P(None, "col", "row"), P(), P(), P(), P(), P("col", "row"), P("col", "row"), P()),
        out_specs=(P(None, "col", "row"), P(), P(), P(), P()),
        check_vma=False,
    )
```

```python
import functools

import jax
import jax.numpy as jnp
from jax import lax
from jax.experimental import pallas as pl
from jax.experimental.pallas import tpu as pltpu
from jax.sharding import PartitionSpec as P

MESH = pl.DeviceIdType.MESH
F32 = jnp.float32
BF16 = jnp.bfloat16
DB = 37
NB = 62
RIM_SEMS = (
    "band_send", "band_recv", "edge_send", "edge_recv", "via_send", "via_recv",
    "relay_send", "corner_send", "corner_recv",
)

def device(x, y, z, core):
    return ((z // 4) * 4 + x, (y * 4 + lax.rem(z, 4)) * 2 + core)


class Place:
    def __init__(self):
        self.row = lax.axis_index("row")
        self.col = lax.axis_index("col")
        self.x = lax.rem(self.row, 4)
        self.core = lax.rem(self.col, 2)
        chip = self.col // 2
        self.y = chip // 4
        self.block = self.row // 4
        self.z = 4 * self.block + lax.rem(chip, 4)
        self.spot = 4 * self.y + self.x

    def mirrors_itself(self):
        return self.spot == self.z

    def mirror_first(self, k):
        return (lax.rem(k, 4), k // 4, self.z, self.core)

    def mirror_second(self, s, half):
        return (lax.rem(self.z, 4), self.z // 4, s, half)

    def plane(self, s):
        return (lax.rem(s // 2, 4), s // 8, self.z, lax.rem(s, 2))

    def plane_slot(self):
        return self.spot * 2 + self.core

    def ring(self, z):
        return (self.x, self.y, z, self.core)


def signal(barrier, target):
    pl.semaphore_signal(barrier, inc=1, device_id=target, device_id_type=MESH)


def next_along_row(me, flow):
    return (me.row + 1, me.col) if flow == 0 else (me.row - 1, me.col)


def near(me, flow):
    return me.x < 3 if flow == 0 else me.x > 0


def far_open(me, flow):
    return me.block < 3 if flow == 0 else me.block > 0


def far_source(flow):
    return 3 if flow == 0 else 0


def far_target(me, flow):
    if flow == 0:
        return device(0, me.y, me.z + 4, me.core)
    return device(3, me.y, me.z - 4, me.core)


def receives(me, flow):
    return me.row > 0 if flow == 0 else me.row < 15


def col_open(me, side):
    return me.col > 0 if side == 0 else me.col < 31


def next_along_col(me, side):
    return (me.row, me.col - 1) if side == 0 else (me.row, me.col + 1)


def greet(me, barrier):
    for side in range(2):
        @pl.when(col_open(me, side))
        def _():
            signal(barrier, next_along_col(me, side))

    for flow in range(2):
        @pl.when(near(me, flow))
        def _():
            signal(barrier, next_along_row(me, flow))

    def far_partners(k, carry):
        @pl.when((me.x == 0) & (me.block > 0))
        def _():
            signal(barrier, device(k, me.y, me.z - 4, me.core))

        @pl.when((me.x == 3) & (me.block < 3))
        def _():
            signal(barrier, device(k, me.y, me.z + 4, me.core))
        return carry

    lax.fori_loop(0, 4, far_partners, 0)

    spot_row, spot_col = (me.z // 4) * 4, 2 * lax.rem(me.z, 4)
    giver_row, giver_col = 4 * me.y, 2 * me.x
    for k in range(16):
        for core in range(2):
            @pl.when(jnp.logical_not((me.spot == k) & (me.core == core)))
            def _():
                signal(barrier, (spot_row + k % 4, spot_col + 8 * (k // 4) + core))

            @pl.when(jnp.logical_not(me.mirrors_itself() & (me.spot == k) & (me.core == core)))
            def _():
                signal(barrier, (giver_row + k % 4, giver_col + 8 * (k // 4) + core))

        @pl.when(me.z != k)
        def _():
            signal(barrier, (me.x + 4 * (k // 4), 8 * me.y + 2 * (k % 4) + me.core))


def await_greetings(me, barrier):
    total = 31 + 15 + 32 - jnp.where(me.mirrors_itself(), 1, 0)
    for k in range(2):
        for known in (col_open(me, k), near(me, k), far_open(me, k)):
            total = total + jnp.where(known, 1, 0)
    pl.semaphore_wait(barrier, total)


def remote(source, target, sent, arrived, to):
    return pltpu.make_async_remote_copy(
        src_ref=source, dst_ref=target, send_sem=sent, recv_sem=arrived,
        device_id=to, device_id_type=MESH,
    )


def edge(refs, flow, k):
    return refs[("right", "left")[flow]].at[pl.ds(2 * k, 2)]


def rim(refs, flow, k):
    return refs[("from_left", "from_right")[flow]].at[pl.ds(2 * k + 2, 2)]


def band_copy(me, refs, sems, side):
    first, into = ((16, 80), (64, 0))[side]
    return remote(
        refs["own"].at[pl.ds(first, 16)], refs["own"].at[pl.ds(into, 16)],
        sems["band_send"].at[side], sems["band_recv"].at[side], next_along_col(me, side),
    )


def edge_copy(me, refs, sems, flow, k, to):
    return remote(
        edge(refs, flow, k), rim(refs, flow, k),
        sems["edge_send"].at[flow, k], sems["edge_recv"].at[flow, k], to,
    )


def via_copy(me, refs, sems, flow, k):
    return remote(
        edge(refs, flow, k), refs["via"].at[flow],
        sems["via_send"].at[flow, k], sems["via_recv"].at[flow],
        device(k, me.y, me.z, me.core),
    )


def relay_copy(me, refs, sems, flow):
    return remote(
        refs["via"].at[flow], rim(refs, flow, me.x),
        sems["relay_send"].at[flow], sems["edge_recv"].at[flow, me.x], far_target(me, flow),
    )


def corner_copy(me, refs, sems, flow, side):
    held = refs[("from_left", "from_right")[flow]]
    first, into = ((2, 10), (8, 0))[side]
    return remote(
        held.at[pl.ds(first, 2)], held.at[pl.ds(into, 2)],
        sems["corner_send"].at[flow, side], sems["corner_recv"].at[flow, side],
        next_along_col(me, side),
    )


def send_rims(me, refs, sems):
    for flow in range(2):
        own = far_source(flow)

        @pl.when((me.x == own) & far_open(me, flow))
        def _():
            for k in range(4):
                if k != own:
                    via_copy(me, refs, sems, flow, k).start()
            edge_copy(me, refs, sems, flow, own, far_target(me, flow)).start()

        @pl.when(near(me, flow))
        def _():
            for k in range(4):
                edge_copy(me, refs, sems, flow, k, next_along_row(me, flow)).start()

    for side in range(2):
        @pl.when(col_open(me, side))
        def _():
            band_copy(me, refs, sems, side).start()

        @pl.when(jnp.logical_not(col_open(me, side)))
        def _():
            into = (0, 80)[side]
            refs["own"][into : into + 16] = jnp.zeros((16, 64, 128), BF16)
            into = (0, 10)[side]
            refs["from_left"][into : into + 2] = jnp.zeros((2, 64, 128), BF16)
            refs["from_right"][into : into + 2] = jnp.zeros((2, 64, 128), BF16)

    for flow in range(2):
        @pl.when(jnp.logical_not(receives(me, flow)))
        def _():
            refs[("from_left", "from_right")[flow]][...] = jnp.zeros((12, 64, 128), BF16)


def relay_rims(me, refs, sems):
    for flow in range(2):
        @pl.when((me.x != far_source(flow)) & far_open(me, flow))
        def _():
            via_copy(me, refs, sems, flow, 0).wait_recv()
            relay_copy(me, refs, sems, flow).start()


def await_rims(me, refs, sems):
    for flow in range(2):
        for k in (0, 3, 1, 2):
            @pl.when(receives(me, flow))
            def _():
                edge_copy(me, refs, sems, flow, k, next_along_row(me, flow)).wait_recv()

            if k in (0, 3):
                side = k // 3

                @pl.when(receives(me, flow) & col_open(me, side))
                def _():
                    corner_copy(me, refs, sems, flow, side).start()

    for side in range(2):
        @pl.when(col_open(me, 1 - side))
        def _():
            band_copy(me, refs, sems, side).wait_recv()

        for flow in range(2):
            @pl.when(receives(me, flow) & col_open(me, 1 - side))
            def _():
                corner_copy(me, refs, sems, flow, side).wait_recv()


def await_sent_rims(me, refs, sems):
    for flow in range(2):
        own = far_source(flow)

        @pl.when((me.x == own) & far_open(me, flow))
        def _():
            for k in range(4):
                if k != own:
                    via_copy(me, refs, sems, flow, k).wait_send()
            edge_copy(me, refs, sems, flow, own, far_target(me, flow)).wait_send()

        @pl.when((me.x != own) & far_open(me, flow))
        def _():
            relay_copy(me, refs, sems, flow).wait_send()

        @pl.when(near(me, flow))
        def _():
            for k in range(4):
                edge_copy(me, refs, sems, flow, k, next_along_row(me, flow)).wait_send()

        for side in range(2):
            @pl.when(receives(me, flow) & col_open(me, side))
            def _():
                corner_copy(me, refs, sems, flow, side).wait_send()

    for side in range(2):
        @pl.when(col_open(me, side))
        def _():
            band_copy(me, refs, sems, side).wait_send()


def lanes():
    return lax.broadcasted_iota(jnp.int32, (64, 128), 1)


def turn(v, by):
    by = by % 128
    return v if by == 0 else pltpu.roll(v, by, 1)


def gather_edges(rows, left, right, at):
    group = lanes() // 16
    low = turn(rows[0], 0)
    high = turn(rows[0], 16)
    for g in range(1, 8):
        low = jnp.where(group == g, turn(rows[g], 16 * g), low)
        high = jnp.where(group == g, turn(rows[g], 16 * (g + 1)), high)
    left[at] = low.astype(BF16)
    right[at] = high.astype(BF16)


def stack_taps(refs, stack, first, last):
    lane = lanes()

    def eight(at, carry):
        before = refs["from_left"][at].astype(F32)
        after = refs["from_right"][at].astype(F32)
        for g in range(8):
            e = at * 8 + g
            cells = refs["own"][e]
            c32 = cells.astype(F32)
            lower = jnp.where(lane < 16, turn(before, -16 * g), turn(c32, 16))
            upper = jnp.where(lane >= 112, turn(after, 112 - 16 * g), turn(c32, 112))
            stack[e, 0:64] = lower.astype(BF16)
            stack[e, 64:128] = cells
            stack[e, 128:192] = upper.astype(BF16)
        return carry

    lax.fori_loop(first, last, eight, 0)


def window(stack, at):
    return jnp.concatenate(
        [
            jnp.concatenate([stack[at * 8 + r + 16 * a] for a in range(3)], axis=0)
            for r in range(8)
        ],
        axis=1,
    )


def rows_of(ref, at):
    return jnp.concatenate([ref[at * 8 + r] for r in range(8)], axis=1)


def strided(i):
    return pl.ds(i, 64, stride=64)


def block(n, at):
    return pl.ds(pl.multiple_of(n * 64 + at * 8, 8), 8)


def kernel(
    feat, cw, cb, wh, hb, dist, omega, mask,
    grad_hbm, sums_out,
    flat, logit, held, own, left, right, from_left, from_right, via, stack, mixed,
    gown, gleft, gright, gfrom_left, gfrom_right, gvia, grads, glogit,
    wc, wf, whp, wht, bias_c, bias_h,
    packed, tmp, placed, sums, rows, src, parts, mine, whole, ring, dst,
    narrowed, leave_sem,
    a_send, a_recv, b_send, b_recv,
    send_1, recv_1, send_2, recv_2, send_3, recv_3,
    *rim_sems,
):
    act_sems = dict(zip(RIM_SEMS, rim_sems[:9]))
    grad_sems = dict(zip(RIM_SEMS, rim_sems[9:]))
    me = Place()
    barrier = pltpu.get_barrier_semaphore()
    greet(me, barrier)
    act = dict(own=own, left=left, right=right, from_left=from_left, from_right=from_right, via=via)
    grd = dict(own=gown, left=gleft, right=gright, from_left=gfrom_left, from_right=gfrom_right, via=gvia)

    def widen(c, carry):
        flat[pl.ds(pl.multiple_of(c * 64, 64), 64), :] = feat[c].astype(F32)
        return carry

    lax.fori_loop(0, 64, widen, 0)

    def activate(at, carry):
        rounded = []
        for g in range(8):
            i = at * 8 + g
            v = flat[strided(i), :]
            held[i] = v.astype(BF16)
            cells = jnp.where(v > 0.0, v, jnp.exp(jnp.minimum(v, 0.0)) - 1.0).astype(BF16)
            own[16 + i] = cells
            rounded.append(cells.astype(F32))
        gather_edges(rounded, left, right, at)
        return carry

    lax.fori_loop(0, 8, activate, 0)
    await_greetings(me, barrier)
    send_rims(me, act, act_sems)

    relay_rims(me, act, act_sems)

    for k in range(9):
        wc[:, 64 * k : 64 * k + 64] = cw[k]
        wf[:, 64 * k : 64 * k + 64] = cw[8 - k].astype(F32).T.astype(BF16)
    whp[...] = jnp.zeros((64, 64), BF16)
    whp[0:NB, :] = wh[...]
    wht[...] = whp[...].astype(F32).T.astype(BF16)
    bias_c[...] = jnp.broadcast_to(cb[...], (128, 64)).T
    bias_h[...] = jnp.zeros((64, 128), F32)
    bias_h[0:NB, :] = jnp.broadcast_to(hb[...], (128, NB)).T

    await_rims(me, act, act_sems)

    def forward(at, carry):
        pre = jnp.dot(wc[...], window(stack, at), preferred_element_type=F32)
        pre = pre + jnp.concatenate([bias_c[...]] * 8, axis=1)
        mix = (rows_of(held, at).astype(F32) + pre).astype(BF16)
        out = jnp.dot(whp[...], mix, preferred_element_type=F32)
        out = (out + jnp.concatenate([bias_h[...]] * 8, axis=1)).astype(BF16).astype(F32)
        for r in range(8):
            mixed[at * 8 + r] = mix[:, 128 * r : 128 * r + 128]
            logit[strided(at * 8 + r), :] = out[:, 128 * r : 128 * r + 128]
        return carry

    def pack(half):
        group = lax.broadcasted_iota(jnp.int32, (32, 128), 1) // 32
        at = 32 * half

        def step(m, carry):
            four = [
                logit[pl.ds(pl.multiple_of(m * 64 + 1024 * q + at, 32), 32), :] for q in range(4)
            ]
            for g in range(4):
                out = turn(four[0], -32 * g)
                for q in range(1, 4):
                    out = jnp.where(group == q, turn(four[q], 32 * (q - g)), out)
                packed[g % 2, m, g // 2, at : at + 32] = out.astype(BF16)
            return carry

        lax.fori_loop(0, 16, step, 0)

    def piece(ref, h, k, part):
        return ref.at[h, lax.rem(part, 2), k, pl.ds(pl.multiple_of(32 * (part // 2), 32), 32)]

    def both(k, part):
        at = pl.ds(pl.multiple_of(32 * (part // 2), 32), 32)
        return packed.at[lax.rem(part, 2), k, :, at]

    apart = lax.rem(me.spot - me.z + 16, 16)
    apart = lax.rem(jnp.minimum(apart, 16 - apart), 8)

    def mirror_a(at, carry):
        part, t = at // 16, lax.rem(at, 16)
        k = lax.rem(apart - t // 2 + 8, 8) + 8 * lax.rem(t, 2)
        to = device(*me.mirror_first(k))

        @pl.when(k == me.spot)
        def _():
            pltpu.make_async_copy(
                both(k, part), tmp.at[part, me.spot], a_recv.at[part, me.spot]
            ).start()

        @pl.when(k != me.spot)
        def _():
            remote(
                both(k, part), tmp.at[part, me.spot],
                a_send.at[part, k], a_recv.at[part, me.spot], to,
            ).start()
        return carry

    def at_home(s, h):
        return me.mirrors_itself() & (s == me.z) & (me.core == h)

    def mirror_b(at, carry):
        part, t = at // 16, lax.rem(at, 16)
        p = lax.rem(me.spot + t // 2, 8)
        back = jnp.where(p == 0, 8, 16 - p)
        s = lax.rem(me.z + jnp.where(lax.rem(t, 2) == 0, p, back), 16)
        pltpu.make_async_copy(both(0, part), tmp.at[part, s], a_recv.at[part, s]).wait()
        for h in range(2):
            @pl.when(at_home(s, h))
            def _():
                pltpu.make_async_copy(
                    tmp.at[part, s, h], piece(placed, me.core, me.spot, part),
                    b_recv.at[part, me.core, me.spot],
                ).start()

            @pl.when(jnp.logical_not(at_home(s, h)))
            def _():
                remote(
                    tmp.at[part, s, h], piece(placed, me.core, me.spot, part),
                    b_send.at[part, s, h], b_recv.at[part, me.core, me.spot],
                    device(*me.mirror_second(s, h)),
                ).start()
        return carry

    stack_taps(act, stack, 0, 8)
    lax.fori_loop(0, 4, forward, 0)
    pack(0)
    lax.fori_loop(0, 32, mirror_a, 0)
    stack_taps(act, stack, 8, 12)

    def forward_and_pass(at, carry):
        forward(at, carry)
        return lax.fori_loop((at - 4) * 8, (at - 3) * 8, mirror_b, carry)

    lax.fori_loop(4, 8, forward_and_pass, 0)
    pack(1)
    lax.fori_loop(32, 64, mirror_a, 0)
    lax.fori_loop(32, 64, mirror_b, 0)

    mine_first = mask[pl.ds(me.col // 2, 1), :].astype(F32)
    mine_first = jnp.broadcast_to(mine_first, (128, 128)).T
    first = jnp.where(me.core == 0, mine_first[0:64], mine_first[64:128])
    pair = first * mask[pl.ds(me.row, 1), :].astype(F32)

    sums[...] = jnp.zeros((3, 64, 128), F32)
    sums[2] = pair
    rows[...] = jnp.zeros((64, 640), F32)

    def arrive(half):
        def step(k, carry):
            for c in range(2):
                for here in range(2):
                    part = 2 * here + half
                    pltpu.make_async_copy(
                        tmp.at[part, 0, 0], piece(placed, c, k, part), b_recv.at[part, c, k]
                    ).wait()
            other = jnp.concatenate([placed[0, half, k], placed[1, half, k]], axis=0)
            other = other.astype(F32).T
            for q in range(4):
                at = pl.ds(pl.multiple_of(k * 64 + 1024 * q + 32 * half, 32), 32)
                flat[at, :] = 0.5 * (logit[at, :] + other[32 * q : 32 * q + 32])
            return carry

        lax.fori_loop(0, 16, step, 0)

    def softmaxes(at, carry):
        eight = pl.ds(pl.multiple_of(at * 8, 8), 8)
        weight = sums[2, eight, :]
        for start, stop, label in ((0, DB, dist), (DB, NB, omega)):
            chosen = label[eight, :]
            top = flat[block(start, at), :]
            for n in range(start + 1, stop):
                top = jnp.maximum(top, flat[block(n, at), :])
            below = jnp.zeros((8, 128), F32)
            for n in range(start, stop):
                e = jnp.exp(flat[block(n, at), :] - top)
                flat[block(n, at), :] = e
                below = below + e
            scale = 1.0 / below
            for n in range(start, stop):
                hot = jnp.where(chosen == n - start, 1.0, 0.0)
                flat[block(n, at), :] = weight * (flat[block(n, at), :] * scale - hot)
        for n in range(NB, 64):
            flat[block(n, at), :] = jnp.zeros((8, 128), F32)
        return carry


    def backward(at, carry):
        per_row = [flat[strided(at * 8 + r), :] for r in range(8)]
        bins = per_row[0]
        for r in range(1, 8):
            bins = bins + per_row[r]
        sums[0] += bins
        for r in range(8):
            glogit[at * 8 + r] = per_row[r].astype(BF16)
        grad_logit = jnp.concatenate([v.astype(BF16) for v in per_row], axis=1)
        back = jnp.dot(wht[...], grad_logit, preferred_element_type=F32)
        pieces = [back[:, 128 * r : 128 * r + 128] for r in range(8)]
        total = pieces[0]
        for r in range(1, 8):
            total = total + pieces[r]
        sums[1] += total
        rounded = []
        for r in range(8):
            grads[at * 8 + r] = pieces[r]
            cells = pieces[r].astype(BF16)
            gown[16 + at * 8 + r] = cells
            rounded.append(cells.astype(F32))
        gather_edges(rounded, gleft, gright, at)
        return carry


    def weights(at, carry):
        over_pairs = (((1,), (1,)), ((), ()))
        rows[:, 0:576] += lax.dot_general(
            jnp.concatenate([gown[16 + at * 8 + r] for r in range(8)], axis=1),
            window(stack, at), over_pairs, preferred_element_type=F32,
        )
        rows[:, 576:640] += lax.dot_general(
            rows_of(glogit, at), rows_of(mixed, at), over_pairs, preferred_element_type=F32
        )
        return carry

    arrive(0)
    lax.fori_loop(0, 4, softmaxes, 0)
    lax.fori_loop(0, 4, backward, 0)
    lax.fori_loop(0, 4, weights, 0)
    arrive(1)
    lax.fori_loop(4, 8, softmaxes, 0)
    lax.fori_loop(4, 8, backward, 0)
    send_rims(me, grd, grad_sems)
    lax.fori_loop(4, 8, weights, 0)
    relay_rims(me, grd, grad_sems)

    rows[62:63, 576:640] = jnp.sum(sums[1].T, axis=0, keepdims=True)
    rows[63:64, 576:640] = jnp.sum(sums[0].T, axis=0, keepdims=True)
    for t in range(5):
        whole[64 * t : 64 * t + 64, :] = rows[:, 128 * t : 128 * t + 128]
    for s in range(32):
        src[s] = whole[10 * s : 10 * s + 10, :]
    slot = me.plane_slot()

    def send_parts(t, carry):
        s = lax.rem(slot + t, 32)
        pltpu.make_async_remote_copy(
            src_ref=src.at[s], dst_ref=parts.at[slot], send_sem=send_1.at[s],
            recv_sem=recv_1.at[slot], device_id=device(*me.plane(s)), device_id_type=MESH,
        ).start()
        return carry

    lax.fori_loop(1, 32, send_parts, 0)
    parts[slot] = src[slot]

    await_sent_rims(me, act, act_sems)

    def sent_mirror(at, carry):
        part, k = at // 16, lax.rem(at, 16)

        @pl.when(k != me.spot)
        def _():
            pltpu.make_async_copy(both(k, part), tmp.at[part, 0], a_send.at[part, k]).wait()

        for h in range(2):
            @pl.when(jnp.logical_not(at_home(k, h)))
            def _():
                pltpu.make_async_copy(
                    tmp.at[part, k, h], piece(placed, 0, 0, part), b_send.at[part, k, h]
                ).wait()
        return carry

    lax.fori_loop(0, 64, sent_mirror, 0)

    def wait_parts(t, carry):
        s = lax.rem(slot + t, 32)
        pltpu.make_async_copy(src.at[0], parts.at[s], recv_1.at[s]).wait()
        return carry

    lax.fori_loop(1, 32, wait_parts, 0)
    mine[0] = jnp.sum(parts[...], axis=0)
    ring[me.z] = mine[0]

    def send_ring(t, carry):
        o = lax.rem(me.z + t, 16)
        pltpu.make_async_remote_copy(
            src_ref=mine.at[0], dst_ref=ring.at[me.z], send_sem=send_2.at[o],
            recv_sem=recv_2.at[me.z], device_id=device(*me.ring(o)), device_id_type=MESH,
        ).start()
        return carry

    lax.fori_loop(1, 16, send_ring, 0)

    await_rims(me, grd, grad_sems)
    stack_taps(grd, stack, 0, 12)

    def inputs(at, carry):
        back = jnp.dot(wf[...], window(stack, at), preferred_element_type=F32)
        for r in range(8):
            i = at * 8 + r
            v = held[i].astype(F32)
            slope = jnp.where(v > 0.0, 1.0, jnp.exp(jnp.minimum(v, 0.0)))
            flat[strided(i), :] = grads[i] + slope * back[:, 128 * r : 128 * r + 128]
        return carry

    lax.fori_loop(0, 4, inputs, 0)

    def wait_ring(t, carry):
        o = lax.rem(me.z + t, 16)
        pltpu.make_async_copy(mine.at[0], ring.at[o], recv_2.at[o]).wait()
        return carry

    lax.fori_loop(1, 16, wait_ring, 0)
    mine[1] = jnp.sum(ring[...], axis=0)
    dst[slot] = mine[1]

    def send_all(t, carry):
        s = lax.rem(slot + t, 32)
        pltpu.make_async_remote_copy(
            src_ref=mine.at[1], dst_ref=dst.at[slot], send_sem=send_3.at[s],
            recv_sem=recv_3.at[slot], device_id=device(*me.plane(s)), device_id_type=MESH,
        ).start()
        return carry

    lax.fori_loop(1, 32, send_all, 0)

    lax.fori_loop(4, 8, inputs, 0)

    def narrow(c, carry):
        narrowed[c] = flat[pl.ds(pl.multiple_of(c * 64, 64), 64), :].astype(BF16)
        return carry

    lax.fori_loop(0, 64, narrow, 0)
    leave = pltpu.make_async_copy(narrowed, grad_hbm, leave_sem.at[0])
    leave.start()
    await_sent_rims(me, grd, grad_sems)

    def sent_sums(t, carry):
        s = lax.rem(slot + t, 32)
        pltpu.make_async_copy(mine.at[0], dst.at[s], send_1.at[s]).wait()
        pltpu.make_async_copy(mine.at[0], dst.at[s], send_3.at[s]).wait()
        return carry

    lax.fori_loop(1, 32, sent_sums, 0)

    def sent_ring(t, carry):
        o = lax.rem(me.z + t, 16)
        pltpu.make_async_copy(mine.at[0], ring.at[o], send_2.at[o]).wait()
        return carry

    lax.fori_loop(1, 16, sent_ring, 0)

    def wait_all(t, carry):
        s = lax.rem(slot + t, 32)
        pltpu.make_async_copy(mine.at[1], dst.at[s], recv_3.at[s]).wait()
        return carry

    lax.fori_loop(1, 32, wait_all, 0)
    for s in range(32):
        sums_out[10 * s : 10 * s + 10, :] = dst[s]
    leave.wait()


def finish(grad, sums, mask, grad_out, cw_out, cb_out, wh_out, hb_out):
    grad_out[...] = grad[...]

    @pl.when(pl.program_id(0) == 0)
    def _():
        count = jnp.sum(mask[...].astype(F32), keepdims=True)
        for k in range(9):
            t, half = k // 2, k % 2
            cw_out[k] = sums[64 * t : 64 * t + 64, 64 * half : 64 * half + 64] / count
        wh_out[...] = sums[256 : 256 + NB, 64:128] / count
        cb_out[...] = sums[318:319, 64:128] / count
        hb_out[...] = sums[319:320, 64 : 64 + NB] / count


def per_device(
    features, conv_weight, conv_bias, head_weight, head_bias, dist_label, omega_label, residue_mask
):
    vmem = pl.BlockSpec(memory_space=pltpu.VMEM)
    cells = (64, 128)
    dma = pltpu.SemaphoreType.DMA
    scratch = [
        pltpu.VMEM((4096, 128), F32),
        pltpu.VMEM((4096, 128), F32),
        pltpu.VMEM((64,) + cells, BF16),
        pltpu.VMEM((96,) + cells, BF16),
        pltpu.VMEM((8,) + cells, BF16),
        pltpu.VMEM((8,) + cells, BF16),
        pltpu.VMEM((12,) + cells, BF16),
        pltpu.VMEM((12,) + cells, BF16),
        pltpu.VMEM((2, 2) + cells, BF16),
        pltpu.VMEM((96, 192, 128), BF16),
        pltpu.VMEM((64,) + cells, BF16),
        pltpu.VMEM((96,) + cells, BF16),
        pltpu.VMEM((8,) + cells, BF16),
        pltpu.VMEM((8,) + cells, BF16),
        pltpu.VMEM((12,) + cells, BF16),
        pltpu.VMEM((12,) + cells, BF16),
        pltpu.VMEM((2, 2) + cells, BF16),
        pltpu.VMEM((64,) + cells, F32),
        pltpu.VMEM((64,) + cells, BF16),
        pltpu.VMEM((64, 576), BF16),
        pltpu.VMEM((64, 576), BF16),
        pltpu.VMEM((64, 64), BF16),
        pltpu.VMEM((64, 64), BF16),
        pltpu.VMEM(cells, F32),
        pltpu.VMEM(cells, F32),
        pltpu.VMEM((2, 16, 2) + cells, BF16),
        pltpu.VMEM((4, 16, 2, 32, 128), BF16),
        pltpu.VMEM((2, 2, 16) + cells, BF16),
        pltpu.VMEM((3,) + cells, F32),
        pltpu.VMEM((64, 640), F32),
        pltpu.VMEM((32, 10, 128), F32),
        pltpu.VMEM((32, 10, 128), F32),
        pltpu.VMEM((2, 10, 128), F32),
        pltpu.VMEM((320, 128), F32),
        pltpu.VMEM((16, 10, 128), F32),
        pltpu.VMEM((32, 10, 128), F32),
        pltpu.VMEM((64,) + cells, BF16),
        dma((1,)),
        dma((4, 16)), dma((4, 16)), dma((4, 16, 2)), dma((4, 2, 16)),
        dma((32,)), dma((32,)), dma((16,)), dma((16,)), dma((32,)), dma((32,)),
    ] + 2 * [
        dma((2,)), dma((2,)), dma((2, 4)), dma((2, 4)), dma((2, 4)), dma((2,)),
        dma((2,)), dma((2, 2)), dma((2, 2)),
    ]
    present = residue_mask.reshape(16, 128)
    grad, sums = pl.pallas_call(
        kernel,
        out_shape=(
            jax.ShapeDtypeStruct(features.shape, BF16),
            jax.ShapeDtypeStruct((320, 128), F32),
        ),
        in_specs=[vmem] * 8,
        out_specs=(pl.BlockSpec(memory_space=pl.ANY), vmem),
        scratch_shapes=scratch,
        compiler_params=pltpu.CompilerParams(collective_id=1, has_side_effects=True),
        name="pair_head",
    )(
        features,
        conv_weight.reshape(9, 64, 64),
        conv_bias.reshape(1, 64),
        head_weight,
        head_bias.reshape(1, NB),
        dist_label,
        omega_label,
        present,
    )
    grad_input, conv_w, conv_b, head_w, head_b = pl.pallas_call(
        finish,
        out_shape=(
            jax.ShapeDtypeStruct(features.shape, BF16),
            jax.ShapeDtypeStruct((9, 64, 64), F32),
            jax.ShapeDtypeStruct((1, 64), F32),
            jax.ShapeDtypeStruct((NB, 64), F32),
            jax.ShapeDtypeStruct((1, NB), F32),
        ),
        grid=(4,),
        in_specs=[
            pl.BlockSpec((16, 64, 128), lambda c: (c, 0, 0)),
            pl.BlockSpec((320, 128), lambda c: (0, 0)),
            pl.BlockSpec((16, 128), lambda c: (0, 0)),
        ],
        out_specs=(
            pl.BlockSpec((16, 64, 128), lambda c: (c, 0, 0)),
            pl.BlockSpec((9, 64, 64), lambda c: (0, 0, 0)),
            pl.BlockSpec((1, 64), lambda c: (0, 0)),
            pl.BlockSpec((NB, 64), lambda c: (0, 0)),
            pl.BlockSpec((1, NB), lambda c: (0, 0)),
        ),
        name="scale",
    )(grad, sums, present)
    return (
        grad_input,
        conv_w.reshape(3, 3, 64, 64),
        conv_b.reshape(64),
        head_w,
        head_b.reshape(NB),
    )


def solution(mesh):
    return jax.shard_map(
        per_device,
        mesh=mesh,
        in_specs=(P(None, "col", "row"), P(), P(), P(), P(), P("col", "row"), P("col", "row"), P()),
        out_specs=(P(None, "col", "row"), P(), P(), P(), P()),
        check_vma=False,
    )
```
